32 devices in a mesh: grp: 2 (over core), aux: 8 (over z, x), tr: 2 (over y).
Axes of the slice: x: 2, y: 2, z: 4, core: 2. Of those that a mesh axis runs over, the one named last changes fastest.
Arguments:
- trial_vectors: float32 [64, 8, 512], P('aux', None, 'tr'), may hold values from -6 to 6
- energy_val: float32 [64], P('aux'), may hold values from -1 to -0.2
- energy_cond: float32 [512], P('tr'), may hold values from 0.2 to 2
- coef_occ: bfloat16 [512, 64, 64], P('aux'), may hold values from -0.75 to 0.75
- coef_virt: bfloat16 [512, 512, 512], P('aux', 'tr'), may hold values from -0.01171875 to 0.01171875
- pair_coef: bfloat16 [64, 512, 512], P('aux', 'tr'), may hold values from -0.03125 to 0.03125
- live_aux: int32 [8], P('aux'), may hold values from 16 to 64, as said below
Outputs:
- applied: float32 [64, 8, 512], P('aux', None, 'tr')
- intersection: float32 [8, 8], replicated
The draws below stay inside these ranges and needn't reach their ends.
Inputs may be any that keep to these rules, and one draw needn't show every extreme that they name: `live_aux`: equals 64 on at least one shard.
All inputs are finite; a program needn't handle non-finite values.
Results may differ from the reference program's by a relative error of at most 0.0048.
Values may be sent and summed in bfloat16 or wider, within the bound.
A program may use at most 64 MiB of HBM per device.

```python
import jax
import jax.numpy as jnp
from jax import lax

V = 64
C = 512
K = 8
PD = 64
NSHARD = 8
NAUX = 512


def draw_live_aux(key, part):
    counts = jax.random.randint(jax.random.fold_in(key, 17), (NSHARD,), PD // 4, PD + 1)
    chosen = jax.random.randint(jax.random.fold_in(key, 29), (), 0, NSHARD)
    return counts.at[chosen].set(PD).astype(jnp.int32)


def block_scale(rng, dims, cuts, least, top_value):
    def one(dim, shards_of):
        draws = jax.random.uniform(jax.random.fold_in(jax.random.fold_in(rng, 6), dim), (shards_of,), jnp.float32, least / len(cuts), top_value / len(cuts))
        return jnp.repeat(jnp.exp(draws), dims[dim] // shards_of).reshape((-1,) + (1,) * (len(dims) - dim - 1))

    loudness = one(*cuts[0])
    for cut in cuts[1:]:
        loudness = loudness * one(*cut)
    return loudness


def bell_draw(key, shape, deviation, bound, cuts=(), held_as=jnp.bfloat16):
    loudness = block_scale(key, shape, cuts, -0.22, 0.18) if cuts else 1.0
    drawn = jax.random.normal(key, shape, jnp.float32) * deviation * loudness
    return jnp.minimum(jnp.maximum(drawn, -bound), bound).astype(held_as)


def setup_inputs(seed: int = 0) -> dict:
    streams_of = jax.random.split(jax.random.key(seed), 8)
    trial_vectors = bell_draw(streams_of[0], (V, K, C), 1.0, 6.0, ((0, 8), (2, 2)), jnp.float32)
    energy_val = jnp.clip(-1.0 + 0.8 * jax.random.uniform(streams_of[1], (V,), jnp.float32) ** block_scale(streams_of[1], (V,), ((0, 8),), -0.2, 0.2), -1.0, -0.2)
    energy_cond = jnp.clip(0.2 + 1.8 * jax.random.uniform(streams_of[2], (C,), jnp.float32) ** block_scale(streams_of[2], (C,), ((0, 2),), -0.2, 0.2), 0.2, 2.0)
    coef_occ = bell_draw(streams_of[3], (NAUX, V, V), V ** -0.5, 0.75, ((0, 8),))
    coef_virt = bell_draw(streams_of[4], (NAUX, C, C), (C * NAUX) ** -0.5, 0.01171875, ((0, 8), (1, 2)))
    pair_coef = bell_draw(streams_of[5], (V, C, NAUX), (V * C) ** -0.5, 0.03125, ((0, 8), (1, 2)))
    live_aux = draw_live_aux(jax.random.fold_in(streams_of[7], 71), 0)
    return dict(trial_vectors=trial_vectors, energy_val=energy_val, energy_cond=energy_cond, coef_occ=coef_occ, coef_virt=coef_virt, pair_coef=pair_coef, live_aux=live_aux)


def apply_hamiltonian(vectors, energy_gap, coef_occ, coef_virt, pair_coef, live_aux):
    rounded = vectors.astype(jnp.bfloat16)
    rounded_wide = rounded.astype(jnp.float32)

    def one_shard(running, shard_index):
        block_occ = lax.dynamic_slice_in_dim(coef_occ, shard_index * PD, PD, 0).astype(jnp.float32)
        block_virt = lax.dynamic_slice_in_dim(coef_virt, shard_index * PD, PD, 0).astype(jnp.float32)
        keep_mask = (jnp.arange(PD, dtype=jnp.int32) < live_aux[shard_index]).astype(jnp.float32)
        blended = jnp.einsum('puv,vkc->pukc', block_occ, rounded_wide)
        blended = (blended * keep_mask[:, None, None, None]).astype(jnp.bfloat16)
        running = running + jnp.einsum('pukc,pcd->ukd', blended.astype(jnp.float32), block_virt)
        return running, None

    zero_term = jnp.zeros((V, K, C), jnp.float32)
    direct_term, _ = lax.scan(one_shard, zero_term, jnp.arange(NSHARD, dtype=jnp.int32))
    pair_wide = pair_coef.astype(jnp.float32)
    projection = jnp.einsum('vcp,vkc->kp', pair_wide, rounded_wide)
    projection_b = projection.astype(jnp.bfloat16)
    exchange_term = jnp.einsum('vcp,kp->vkc', pair_wide, projection_b.astype(jnp.float32))
    return energy_gap[:, None, :] * vectors + direct_term + exchange_term


def reference(trial_vectors, energy_val, energy_cond, coef_occ, coef_virt, pair_coef, live_aux):
    energy_gap = energy_cond[None, :] - energy_val[:, None]
    applied_first = apply_hamiltonian(trial_vectors, energy_gap, coef_occ, coef_virt, pair_coef, live_aux)
    intersection = jnp.einsum('vkc,vjc->kj', trial_vectors, applied_first, precision=lax.Precision.HIGHEST) / (V * C)
    residual = applied_first - jnp.einsum('vkc,kj->vjc', trial_vectors, intersection, precision=lax.Precision.HIGHEST)
    correction = residual / energy_gap[:, None, :]
    applied = apply_hamiltonian(correction, energy_gap, coef_occ, coef_virt, pair_coef, live_aux)
    return applied, intersection
```

```python
import contextlib
import functools

import jax
import jax.numpy as jnp
from jax import lax
from jax.experimental import pallas as pl
from jax.experimental.pallas import tpu as pltpu
from jax.sharding import PartitionSpec as P

F32 = jnp.float32
BF16 = jnp.bfloat16
CHUNK = 32
BLEND = 32
LANES = 128
MESH = pl.DeviceIdType.MESH


def scope(name):
    return contextlib.nullcontext()


def kernel(
    naux, ntr,
    live_ref, trial_ref, val_ref, cond_ref, occ_hbm, virt_hbm, pair_hbm,
    out_ref, inter_ref,
    occ, virt, pair, blended, acc, mixed, trial_k,
    block_send, block_recv, mate_recv, proj_send, proj_recv, tr_send, tr_recv,
    sum_send, sum_recv, dots_send, dots_recv, core_recv, final_send, final_recv,
    load_sem, block_ssem, block_rsem, mate_sem, proj_ssem, proj_rsem,
    tr_ssem, tr_rsem, sum_ssem, sum_rsem, dots_ssem, dots_rsem, core_ssem, core_rsem,
):
    g = lax.axis_index("grp")
    a = lax.axis_index("aux")
    t = lax.axis_index("tr")
    own_val, vectors, cond = trial_ref.shape
    half = vectors // 2
    slots, val, _ = occ.shape

    pair_copy = pltpu.make_async_copy(pair_hbm, pair, load_sem.at[1])
    occ_copy = pltpu.make_async_copy(occ_hbm, occ, load_sem.at[0])
    virt_copy = pltpu.make_async_copy(virt_hbm, virt, load_sem.at[2])

    everyone = [(da, dt) for da in range(naux) for dt in range(ntr) if (da, dt) != (0, 0)]

    def peer(da, dt):
        return {"aux": lax.rem(a + da, naux), "tr": lax.rem(t + dt, ntr)}

    barrier = pltpu.get_barrier_semaphore()
    with scope("signals"):
        for da, dt in everyone:
            pl.semaphore_signal(barrier, inc=1, device_id=peer(da, dt), device_id_type=MESH)
        pl.semaphore_signal(barrier, inc=1, device_id={"grp": 1 - g}, device_id_type=MESH)
    pair_copy.start()
    occ_copy.start()
    virt_copy.start()

    with scope("prep"):
        square = (own_val, own_val)
        diagonal = lax.broadcasted_iota(jnp.int32, square, 0) == lax.broadcasted_iota(jnp.int32, square, 1)
        val_column = jnp.sum(jnp.where(diagonal, val_ref[...], 0.0), axis=1, keepdims=True)
        gap = cond_ref[...] - val_column
        for k in range(vectors):
            trial_k[k] = trial_ref[:, k, :]

    def to_all(it, send, recv, ssem, rsem):
        copies = []
        for da, dt in everyone:
            n = da * ntr + dt
            copies.append(pltpu.make_async_remote_copy(
                src_ref=send.at[it], dst_ref=recv.at[it, n],
                send_sem=ssem.at[it, n], recv_sem=rsem.at[it, n],
                device_id=peer(da, dt), device_id_type=MESH))
        return copies

    mate = pltpu.make_async_remote_copy(
        src_ref=block_recv.at[0], dst_ref=mate_recv,
        send_sem=mate_sem.at[0], recv_sem=mate_sem.at[1],
        device_id={"grp": 1 - g}, device_id_type=MESH)

    def contract(cols):
        acc[...] = jnp.zeros_like(acc)

        @pl.loop(0, slots // CHUNK)
        def _(i):
            acc[...] += jnp.dot(
                blended[i], virt[pl.ds(i * CHUNK, CHUNK), :, cols].reshape(CHUNK * cond, cond),
                preferred_element_type=F32)

    lanes = lax.broadcasted_iota(jnp.int32, (vectors, LANES), 1)

    def fold(x):
        return sum(x[:, n * LANES:(n + 1) * LANES] for n in range(cond // LANES))

    def overlaps(local):
        mine = [[fold(local[j] * trial_k[k]) for k in range(vectors)] for j in range(half)]
        for s in range(naux):
            same = block_recv[0, s].astype(F32)
            other = mate_recv[s].astype(F32)
            for j in range(half):
                row = j * val + s * own_val
                part = acc[row:row + own_val, :]
                for k in range(half):
                    where = slice(k * cond, (k + 1) * cond)
                    mine[j][k] += fold(part * jnp.where(g == 0, same[:, where], other[:, where]))
                    mine[j][half + k] += fold(part * jnp.where(g == 0, other[:, where], same[:, where]))
        partial = jnp.zeros((vectors, LANES), F32)
        for j in range(half):
            rows = jnp.concatenate([jnp.sum(m, axis=0, keepdims=True) for m in mine[j]], axis=0)
            partial += jnp.where(lanes == g * half + j, jnp.sum(rows, axis=1, keepdims=True), 0.0)
        return partial

    def apply(it, x):
        with scope("pack"):
            block = jnp.concatenate(x, axis=1).astype(BF16)
            block_send[it] = block
            block_recv[it, a] = block
        if it == 0:
            with scope("barrier"):
                pl.semaphore_wait(barrier, len(everyone) + 1)
        gathers = []
        with scope("gather_issue"):
            for d in range(1, naux):
                copy = pltpu.make_async_remote_copy(
                    src_ref=block_send.at[it], dst_ref=block_recv.at[it, a],
                    send_sem=block_ssem.at[it, d], recv_sem=block_rsem.at[it, d],
                    device_id=peer(d, 0), device_id_type=MESH)
                copy.start()
                gathers.append(copy)

        with scope("project"):
            if it == 0:
                pair_copy.wait()
            for k in range(half):
                mixed[:, k, :] = x[k]
            proj = jnp.zeros((half, pair.shape[2]), F32)
            for v in range(own_val):
                proj += jnp.dot(mixed[v].astype(BF16), pair[v], preferred_element_type=F32)
            proj_send[it] = proj.astype(BF16)
            projections = to_all(it, proj_send, proj_recv, proj_ssem, proj_rsem)
            for copy in projections:
                copy.start()

        if it == 0:
            with scope("mask"):
                occ_copy.wait()
                live = live_ref[...]
                step = min(16, slots)

                @pl.loop(0, slots // step)
                def _(i):
                    for q in range(step):
                        p = i * step + q
                        keep = jnp.broadcast_to((p < live).astype(F32), (val, val)).astype(BF16)
                        occ[p] = occ[p] * keep

        with scope("gather_wait"):
            for copy in gathers:
                copy.wait_recv()
        if it == 0:
            mate.start()
        with scope("blend"):
            wide = jnp.concatenate([block_recv[it, s].astype(F32) for s in range(naux)], axis=0).astype(BF16)
            columns = [wide[:, k * cond:(k + 1) * cond] for k in range(half)]

            @pl.loop(0, slots // BLEND)
            def _(i):
                rows = occ[pl.ds(i * BLEND, BLEND)].reshape(BLEND * val, val)
                for k in range(half):
                    b = jnp.dot(rows, columns[k], preferred_element_type=F32).astype(BF16)
                    for q in range(BLEND):
                        blended[i * (BLEND // CHUNK) + q // CHUNK, k * val:(k + 1) * val,
                                (q % CHUNK) * cond:(q % CHUNK + 1) * cond] = b[q * val:(q + 1) * val]

        if it == 0:
            with scope("virt_wait"):
                virt_copy.wait()
        tr_copy = pltpu.make_async_remote_copy(
            src_ref=tr_send.at[it], dst_ref=tr_recv.at[it],
            send_sem=tr_ssem.at[it], recv_sem=tr_rsem.at[it],
            device_id=peer(0, 1), device_id_type=MESH)

        with scope("contract"):
            @pl.loop(0, 2)
            def _(j):
                start = pl.multiple_of(lax.rem(t + 1 + j, ntr) * cond, cond)
                contract(pl.ds(start, cond))

                @pl.when(j == 0)
                def _():
                    tr_send[it] = acc[...].astype(BF16)
                    tr_copy.start()

        with scope("exchange"):
            for copy in projections:
                copy.wait_recv()
            proj = proj_send[it].astype(F32)
            for da, dt in everyone:
                proj += proj_recv[it, da * ntr + dt].astype(F32)
            proj_b = proj.astype(BF16)
            for v in range(own_val):
                mixed[v] = lax.dot_general(
                    proj_b, pair[v], (((1,), (1,)), ((), ())), preferred_element_type=F32)
            local = [gap * x[k] + mixed[:, k, :] for k in range(half)]

        with scope("tr_wait"):
            if it == 0:
                mate.wait_recv()
            tr_copy.wait_recv()
        dots = []
        partial = None
        with scope("dots_calc"):
            acc[...] += tr_recv[it].astype(F32)
            if it == 0:
                partial = overlaps(local)
                dots_send[0] = partial
                dots = to_all(0, dots_send, dots_recv, dots_ssem, dots_rsem)
                for copy in dots:
                    copy.start()

        sums = []
        with scope("sum_issue"):
            for s in range(naux):
                for k in range(half):
                    row = k * val + s * own_val
                    sum_send[it, s, :, k * cond:(k + 1) * cond] = acc[row:row + own_val, :].astype(BF16)
            for d in range(1, naux):
                copy = pltpu.make_async_remote_copy(
                    src_ref=sum_send.at[it, lax.rem(a + d, naux)], dst_ref=sum_recv.at[it, d],
                    send_sem=sum_ssem.at[it, d], recv_sem=sum_rsem.at[it, d],
                    device_id=peer(d, 0), device_id_type=MESH)
                copy.start()
                sums.append(copy)
        with scope("sum_wait"):
            for copy in sums:
                copy.wait_recv()
        with scope("combine"):
            total = sum_send[it, a].astype(F32)
            for d in range(1, naux):
                total += sum_recv[it, d].astype(F32)
            result = [local[k] + total[:, k * cond:(k + 1) * cond] for k in range(half)]
        sent = gathers + projections + sums + [tr_copy] + ([mate] if it == 0 else [])
        return result, partial, dots, sent

    first, partial, dots, sent = apply(0, [trial_k[g * half + k] for k in range(half)])

    with scope("dots_wait"):
        for copy in dots:
            copy.wait_recv()
    with scope("correct"):
        for da, dt in everyone:
            partial += dots_recv[0, da * ntr + dt]
        inter = partial / (naux * own_val * ntr * cond)
        dots_send[1] = inter
        core_dots = pltpu.make_async_remote_copy(
            src_ref=dots_send.at[1], dst_ref=core_recv,
            send_sem=core_ssem.at[0], recv_sem=core_rsem.at[0],
            device_id={"grp": 1 - g}, device_id_type=MESH)
        core_dots.start()

        correction = []
        for j in range(half):
            column = jnp.sum(jnp.where(lanes == g * half + j, inter, 0.0), axis=1, keepdims=True)
            fitted = trial_k[0] * column[0:1, :]
            for k in range(1, vectors):
                fitted += trial_k[k] * column[k:k + 1, :]
            correction.append((first[j] - fitted) / gap)

    second, _, _, sent_second = apply(1, correction)
    with scope("final_pack"):
        for k in range(half):
            final_send[k] = second[k]
        final_copy = pltpu.make_async_remote_copy(
            src_ref=final_send, dst_ref=final_recv,
            send_sem=core_ssem.at[1], recv_sem=core_rsem.at[1],
            device_id={"grp": 1 - g}, device_id_type=MESH)
        final_copy.start()
        for k in range(half):
            out_ref[g * half + k] = second[k]
    with scope("final_sends"):
        core_dots.wait()
        inter_ref[...] = (dots_send[1] + core_recv[...])[:, :vectors]
        for copy in sent + dots + sent_second:
            copy.wait_send()
    with scope("final_wait"):
        final_copy.wait()
    with scope("final_store"):
        for k in range(half):
            out_ref[(1 - g) * half + k] = final_recv[k]


def finish(applied_ref, inter_ref, out_ref, inter_out_ref):
    for k in range(applied_ref.shape[0]):
        out_ref[:, k, :] = applied_ref[k]
    inter_out_ref[...] = inter_ref[...]


def body(naux, ntr, trial_vectors, energy_val, energy_cond, coef_occ, coef_virt, pair_coef, live_aux):
    own_val, vectors, cond = trial_vectors.shape
    slots, val, _ = coef_occ.shape
    naux_all = pair_coef.shape[2]
    half = vectors // 2
    peers = naux * ntr
    vmem = pl.BlockSpec(memory_space=pltpu.VMEM)
    hbm = pl.BlockSpec(memory_space=pl.ANY)
    dma = pltpu.SemaphoreType.DMA
    scratch = [
        pltpu.VMEM(coef_occ.shape, BF16),
        pltpu.VMEM(coef_virt.shape, BF16),
        pltpu.VMEM(pair_coef.shape, BF16),
        pltpu.VMEM((slots // CHUNK, half * val, CHUNK * cond), BF16),
        pltpu.VMEM((half * val, cond), F32),
        pltpu.VMEM((own_val, half, cond), F32),
        pltpu.VMEM((vectors, own_val, cond), F32),
        pltpu.VMEM((2, own_val, half * cond), BF16),
        pltpu.VMEM((2, naux, own_val, half * cond), BF16),
        pltpu.VMEM((naux, own_val, half * cond), BF16),
        pltpu.VMEM((2, half, naux_all), BF16),
        pltpu.VMEM((2, peers, half, naux_all), BF16),
        pltpu.VMEM((2, half * val, cond), BF16),
        pltpu.VMEM((2, half * val, cond), BF16),
        pltpu.VMEM((2, naux, own_val, half * cond), BF16),
        pltpu.VMEM((2, naux, own_val, half * cond), BF16),
        pltpu.VMEM((2, vectors, LANES), F32),
        pltpu.VMEM((1, peers, vectors, LANES), F32),
        pltpu.VMEM((vectors, LANES), F32),
        pltpu.VMEM((half, own_val, cond), F32),
        pltpu.VMEM((half, own_val, cond), F32),
        dma((3,)),
        dma((2, naux)), dma((2, naux)),
        dma((2,)),
        dma((2, peers)), dma((2, peers)),
        dma((2,)), dma((2,)),
        dma((2, naux)), dma((2, naux)),
        dma((1, peers)), dma((1, peers)),
        dma((2,)), dma((2,)),
    ]
    applied, intersection = pl.pallas_call(
        functools.partial(kernel, naux, ntr),
        out_shape=(
            jax.ShapeDtypeStruct((vectors, own_val, cond), F32),
            jax.ShapeDtypeStruct((vectors, vectors), F32),
        ),
        in_specs=[vmem, vmem, vmem, vmem, hbm, hbm, hbm],
        out_specs=(vmem, vmem),
        scratch_shapes=scratch,
        compiler_params=pltpu.CompilerParams(
            collective_id=0, has_side_effects=True, vmem_limit_bytes=56 * 1024 * 1024
        ),
    )(
        live_aux.reshape(1, 1), trial_vectors, energy_val.reshape(1, -1),
        energy_cond.reshape(1, -1), coef_occ, coef_virt, pair_coef,
    )
    return pl.pallas_call(
        finish,
        out_shape=(
            jax.ShapeDtypeStruct(trial_vectors.shape, F32),
            jax.ShapeDtypeStruct((vectors, vectors), F32),
        ),
        in_specs=[vmem, vmem],
        out_specs=(vmem, vmem),
    )(applied, intersection)


def solution(mesh):
    in_specs = (
        P("aux", None, "tr"),
        P("aux"),
        P("tr"),
        P("aux", None, None),
        P("aux", "tr", None),
        P("aux", "tr", None),
        P("aux"),
    )
    out_specs = (P("aux", None, "tr"), P())
    sizes = (mesh.shape["aux"], mesh.shape["tr"])
    return jax.shard_map(
        functools.partial(body, *sizes), mesh=mesh, in_specs=in_specs, out_specs=out_specs, check_vma=False
    )
```

```python
import contextlib
import functools

import jax
import jax.numpy as jnp
from jax import lax
from jax.experimental import pallas as pl
from jax.experimental.pallas import tpu as pltpu
from jax.sharding import PartitionSpec as P

F32 = jnp.float32
BF16 = jnp.bfloat16
CHUNK = 32
BLEND = 32
LANES = 128
MESH = pl.DeviceIdType.MESH


def scope(name):
    return contextlib.nullcontext()


def kernel(
    naux, ntr,
    live_ref, trial_ref, val_ref, cond_ref, occ_hbm, virt_hbm, pair_hbm,
    out_ref, inter_ref,
    occ, virt, pair, blended, acc, mixed, trial_k, own_row,
    block_send, block_recv, cross_recv, mate_recv, proj_send, proj_recv, proj_all, proj_mate,
    sum_send, sum_recv, dots_send, dots_recv, core_recv, final_send, final_recv,
    load_sem, block_ssem, block_rsem, extra_ssem, extra_rsem, proj_ssem, proj_rsem,
    sum_ssem, sum_rsem, dots_ssem, dots_rsem, core_ssem, core_rsem,
):
    g = lax.axis_index("grp")
    a = lax.axis_index("aux")
    t = lax.axis_index("tr")
    own_val, vectors, cond = trial_ref.shape
    half = vectors // 2
    slots, val, _ = occ.shape
    here = a * ntr + t

    pair_copy = pltpu.make_async_copy(pair_hbm, pair, load_sem.at[1])
    occ_copy = pltpu.make_async_copy(occ_hbm, occ, load_sem.at[0])
    virt_copy = pltpu.make_async_copy(virt_hbm, virt, load_sem.at[2])

    everyone = [(da, dt) for da in range(naux) for dt in range(ntr) if (da, dt) != (0, 0)]

    def peer(da, dt):
        return {"aux": lax.rem(a + da, naux), "tr": lax.rem(t + dt, ntr)}

    def send(src, dst, ssem, rsem, device):
        return pltpu.make_async_remote_copy(
            src_ref=src, dst_ref=dst, send_sem=ssem, recv_sem=rsem, device_id=device, device_id_type=MESH)

    mate = {"grp": 1 - g}
    barrier = pltpu.get_barrier_semaphore()
    with scope("signals"):
        for da, dt in everyone:
            pl.semaphore_signal(barrier, inc=1, device_id=peer(da, dt), device_id_type=MESH)
        pl.semaphore_signal(barrier, inc=1, device_id=mate, device_id_type=MESH)
    pair_copy.start()
    occ_copy.start()
    virt_copy.start()

    with scope("prep"):
        square = (own_val, own_val)
        diagonal = lax.broadcasted_iota(jnp.int32, square, 0) == lax.broadcasted_iota(jnp.int32, square, 1)
        val_column = jnp.sum(jnp.where(diagonal, val_ref[...], 0.0), axis=1, keepdims=True)
        gap = cond_ref[...] - val_column
        for k in range(vectors):
            trial_k[k] = trial_ref[:, k, :]

    pairs = half * vectors
    lane = lax.broadcasted_iota(jnp.int32, (vectors, LANES), 1)
    vector = lax.broadcasted_iota(jnp.int32, (vectors, LANES), 0)

    def fold(x):
        return sum(x[:, n * LANES:(n + 1) * LANES] for n in range(x.shape[1] // LANES))

    def row_of(parts):
        rows = jnp.concatenate([jnp.sum(p, axis=0, keepdims=True) for part in parts for p in part], axis=0)
        n = lax.broadcasted_iota(jnp.int32, (pairs, LANES), 0)
        j = n // vectors
        place = j * vectors + lax.rem(n - j * vectors + g * half, vectors)
        spread = lax.broadcasted_iota(jnp.int32, (pairs, LANES), 1) == place
        return jnp.sum(jnp.where(spread, jnp.sum(rows, axis=1, keepdims=True), 0.0), axis=0, keepdims=True)

    def column(row, j):
        return jnp.sum(jnp.where(lane == j * vectors + vector, row, 0.0), axis=1, keepdims=True)

    def contract(cols):
        acc[...] = jnp.zeros_like(acc)

        @pl.loop(0, slots // CHUNK)
        def _(i):
            acc[...] += jnp.dot(
                blended[i], virt[pl.ds(i * CHUNK, CHUNK), :, cols].reshape(CHUNK * cond, cond),
                preferred_element_type=F32)

    def apply(it, x):
        started = []

        def go(copy):
            copy.start()
            started.append(copy)
            return copy

        with scope("pack"):
            block = jnp.concatenate(x, axis=1).astype(BF16)
            block_send[it] = block
            block_recv[it, a] = block
        if it == 0:
            with scope("barrier"):
                pl.semaphore_wait(barrier, len(everyone) + 1)
        with scope("gather_issue"):
            gathers = [
                go(send(block_send.at[it], block_recv.at[it, a], block_ssem.at[it, d], block_rsem.at[it, d], peer(d, 0)))
                for d in range(1, naux)]

        with scope("project"):
            if it == 0:
                pair_copy.wait()
            for k in range(half):
                mixed[:, k, :] = x[k]
            proj = jnp.zeros((half, pair.shape[2]), F32)
            for v in range(own_val):
                proj += jnp.dot(mixed[v].astype(BF16), pair[v], preferred_element_type=F32)
            proj_send[it] = proj.astype(BF16)
            proj_recv[it, here] = proj.astype(BF16)

        if it == 0:
            with scope("mask"):
                occ_copy.wait()
                live = live_ref[...]
                step = min(16, slots)

                @pl.loop(0, slots // step)
                def _(i):
                    for q in range(step):
                        p = i * step + q
                        keep = jnp.broadcast_to((p < live).astype(F32), (val, val)).astype(BF16)
                        occ[p] = occ[p] * keep

                others = [trial_k[lax.rem(g * half + n, vectors)] for n in range(vectors)]
                own_row[...] = row_of([[fold(gap * others[j] * others[n]) for n in range(vectors)] for j in range(half)])

        with scope("gather_wait"):
            for copy in gathers:
                copy.wait_recv()
        if it == 0:
            mate_cross = send(cross_recv, mate_recv.at[1], extra_ssem.at[2], extra_rsem.at[2], mate)
        with scope("proj_issue"):
            projections = []
            for da, dt in everyone:
                n = da * ntr + dt
                projections.append(go(send(
                    proj_send.at[it], proj_recv.at[it, here], proj_ssem.at[it, n], proj_rsem.at[it, n], peer(da, dt))))
            if it == 0:
                mate_own = go(send(block_recv.at[0], mate_recv.at[0], extra_ssem.at[0], extra_rsem.at[0], mate))
                cross = go(send(block_recv.at[0], cross_recv, extra_ssem.at[1], extra_rsem.at[1], peer(0, 1)))
        with scope("blend"):
            wide = jnp.concatenate([block_recv[it, s].astype(F32) for s in range(naux)], axis=0).astype(BF16)
            columns = [wide[:, k * cond:(k + 1) * cond] for k in range(half)]

            @pl.loop(0, slots // BLEND)
            def _(i):
                rows = occ[pl.ds(i * BLEND, BLEND)].reshape(BLEND * val, val)
                for k in range(half):
                    b = jnp.dot(rows, columns[k], preferred_element_type=F32).astype(BF16)
                    for q in range(BLEND):
                        blended[i * (BLEND // CHUNK) + q // CHUNK, k * val:(k + 1) * val,
                                (q % CHUNK) * cond:(q % CHUNK + 1) * cond] = b[q * val:(q + 1) * val]

        if it == 0:
            with scope("virt_wait"):
                virt_copy.wait()

        def sum_copies(dt):
            return [
                send(sum_send.at[it, dt, lax.rem(a + d, naux)], sum_recv.at[it, dt, d],
                     sum_ssem.at[it, dt, d], sum_rsem.at[it, dt, d], peer(d, dt))
                for d in range(1 - dt, naux)]

        with scope("contract"):
            @pl.loop(0, 2)
            def _(j):
                start = pl.multiple_of(lax.rem(t + 1 - j, ntr) * cond, cond)
                contract(pl.ds(start, cond))
                for s in range(naux):
                    for k in range(half):
                        row = k * val + s * own_val
                        sum_send[it, 1 - j, s, :, k * cond:(k + 1) * cond] = acc[row:row + own_val, :].astype(BF16)

                @pl.when(j == 0)
                def _():
                    for copy in sum_copies(1):
                        copy.start()
                    if it == 0:
                        cross.wait_recv()
                        mate_cross.start()

        with scope("sum_issue"):
            for copy in sum_copies(0):
                copy.start()
            sums = sum_copies(1) + sum_copies(0)
            started.extend(sums + ([mate_cross] if it == 0 else []))

        dots = []
        if it == 0:
            with scope("overlap"):
                mate_own.wait_recv()
                mate_cross.wait_recv()
                parts = [[jnp.zeros((own_val, LANES), F32)] * vectors for _ in range(half)]
                for dt in range(2):
                    for s in range(naux):
                        part = sum_send[0, dt, s].astype(F32)
                        same = (block_recv[0, s] if dt == 0 else cross_recv[s]).astype(F32)
                        other = mate_recv[dt, s].astype(F32)
                        both = [y[:, k * cond:(k + 1) * cond] for y in (same, other) for k in range(half)]
                        for j in range(half):
                            mine = part[:, j * cond:(j + 1) * cond]
                            for n in range(vectors):
                                parts[j][n] = parts[j][n] + fold(mine * both[n])
                row = own_row[...] + row_of(parts)
                dots_send[...] = row
                dots_recv[here] = row
            with scope("dots_issue"):
                for da, dt in everyone:
                    n = da * ntr + dt
                    dots.append(go(send(dots_send, dots_recv.at[here], dots_ssem.at[n], dots_rsem.at[n], peer(da, dt))))

        with scope("exchange"):
            for copy in projections:
                copy.wait_recv()
            proj = proj_recv[it, 0].astype(F32)
            for n in range(1, naux * ntr):
                proj += proj_recv[it, n].astype(F32)
            if it == 0:
                proj_all[...] = proj
                mate_proj = go(send(proj_all, proj_mate, extra_ssem.at[3], extra_rsem.at[3], mate))
            proj_b = proj.astype(BF16)
            for v in range(own_val):
                mixed[v] = lax.dot_general(
                    proj_b, pair[v], (((1,), (1,)), ((), ())), preferred_element_type=F32)
            local = [gap * x[k] + mixed[:, k, :] for k in range(half)]

        with scope("sum_wait"):
            for copy in sums:
                copy.wait_recv()
        with scope("combine"):
            total = sum_send[it, 0, a].astype(F32)
            for dt in range(2):
                for d in range(1 - dt, naux):
                    total += sum_recv[it, dt, d].astype(F32)
            result = [local[k] + total[:, k * cond:(k + 1) * cond] for k in range(half)]
        return result, dots, proj_b, mate_proj if it == 0 else None, started

    first, dots, proj_b, mate_proj, started = apply(0, [trial_k[g * half + k] for k in range(half)])

    with scope("dots_wait"):
        mate_proj.wait_recv()
        for copy in dots:
            copy.wait_recv()
    with scope("correct"):
        row = dots_recv[0]
        for n in range(1, naux * ntr):
            row += dots_recv[n]
        both = jnp.concatenate([proj_all[...], proj_mate[...]], axis=0)
        both = jnp.where(g == 0, both, jnp.concatenate([proj_mate[...], proj_all[...]], axis=0))
        inter = []
        for j in range(half):
            exchanged = jnp.sum(fold(both * proj_b[j:j + 1].astype(F32)), axis=1, keepdims=True)
            inter.append((column(row, j) + exchanged) / (naux * own_val * ntr * cond))
        square = jnp.zeros((vectors, LANES), F32)
        for j in range(half):
            square += jnp.where(lane == g * half + j, inter[j], 0.0)
        core_recv[0] = square
        core_dots = send(core_recv.at[0], core_recv.at[1], core_ssem.at[0], core_rsem.at[0], mate)
        core_dots.start()

        correction = []
        for j in range(half):
            fitted = trial_k[0] * inter[j][0:1, :]
            for k in range(1, vectors):
                fitted += trial_k[k] * inter[j][k:k + 1, :]
            correction.append((first[j] - fitted) / gap)

    second, _, _, _, started_second = apply(1, correction)
    with scope("final_pack"):
        for k in range(half):
            final_send[k] = second[k]
        final_copy = send(final_send, final_recv, core_ssem.at[1], core_rsem.at[1], mate)
        final_copy.start()
        for k in range(half):
            out_ref[g * half + k] = second[k]
    with scope("final_sends"):
        core_dots.wait()
        inter_ref[...] = (core_recv[0] + core_recv[1])[:, :vectors]
        for copy in started + started_second:
            copy.wait_send()
    with scope("final_wait"):
        final_copy.wait()
    with scope("final_store"):
        for k in range(half):
            out_ref[(1 - g) * half + k] = final_recv[k]


def finish(applied_ref, inter_ref, out_ref, inter_out_ref):
    for k in range(applied_ref.shape[0]):
        out_ref[:, k, :] = applied_ref[k]
    inter_out_ref[...] = inter_ref[...]


def body(naux, ntr, trial_vectors, energy_val, energy_cond, coef_occ, coef_virt, pair_coef, live_aux):
    own_val, vectors, cond = trial_vectors.shape
    slots, val, _ = coef_occ.shape
    naux_all = pair_coef.shape[2]
    half = vectors // 2
    peers = naux * ntr
    vmem = pl.BlockSpec(memory_space=pltpu.VMEM)
    hbm = pl.BlockSpec(memory_space=pl.ANY)
    dma = pltpu.SemaphoreType.DMA
    block = (own_val, half * cond)
    scratch = [
        pltpu.VMEM(coef_occ.shape, BF16),
        pltpu.VMEM(coef_virt.shape, BF16),
        pltpu.VMEM(pair_coef.shape, BF16),
        pltpu.VMEM((slots // CHUNK, half * val, CHUNK * cond), BF16),
        pltpu.VMEM((half * val, cond), F32),
        pltpu.VMEM((own_val, half, cond), F32),
        pltpu.VMEM((vectors, own_val, cond), F32),
        pltpu.VMEM((1, LANES), F32),
        pltpu.VMEM((2, *block), BF16),
        pltpu.VMEM((2, naux, *block), BF16),
        pltpu.VMEM((naux, *block), BF16),
        pltpu.VMEM((2, naux, *block), BF16),
        pltpu.VMEM((2, half, naux_all), BF16),
        pltpu.VMEM((2, peers, half, naux_all), BF16),
        pltpu.VMEM((half, naux_all), F32),
        pltpu.VMEM((half, naux_all), F32),
        pltpu.VMEM((2, 2, naux, *block), BF16),
        pltpu.VMEM((2, 2, naux, *block), BF16),
        pltpu.VMEM((1, LANES), F32),
        pltpu.VMEM((peers, 1, LANES), F32),
        pltpu.VMEM((2, vectors, LANES), F32),
        pltpu.VMEM((half, own_val, cond), F32),
        pltpu.VMEM((half, own_val, cond), F32),
        dma((3,)),
        dma((2, naux)), dma((2, naux)),
        dma((4,)), dma((4,)),
        dma((2, peers)), dma((2, peers)),
        dma((2, 2, naux)), dma((2, 2, naux)),
        dma((peers,)), dma((peers,)),
        dma((2,)), dma((2,)),
    ]
    applied, intersection = pl.pallas_call(
        functools.partial(kernel, naux, ntr),
        out_shape=(
            jax.ShapeDtypeStruct((vectors, own_val, cond), F32),
            jax.ShapeDtypeStruct((vectors, vectors), F32),
        ),
        in_specs=[vmem, vmem, vmem, vmem, hbm, hbm, hbm],
        out_specs=(vmem, vmem),
        scratch_shapes=scratch,
        compiler_params=pltpu.CompilerParams(
            collective_id=0, has_side_effects=True, vmem_limit_bytes=56 * 1024 * 1024
        ),
    )(
        live_aux.reshape(1, 1), trial_vectors, energy_val.reshape(1, -1),
        energy_cond.reshape(1, -1), coef_occ, coef_virt, pair_coef,
    )
    return pl.pallas_call(
        finish,
        out_shape=(
            jax.ShapeDtypeStruct(trial_vectors.shape, F32),
            jax.ShapeDtypeStruct((vectors, vectors), F32),
        ),
        in_specs=[vmem, vmem],
        out_specs=(vmem, vmem),
    )(applied, intersection)


def solution(mesh):
    in_specs = (
        P("aux", None, "tr"),
        P("aux"),
        P("tr"),
        P("aux", None, None),
        P("aux", "tr", None),
        P("aux", "tr", None),
        P("aux"),
    )
    out_specs = (P("aux", None, "tr"), P())
    sizes = (mesh.shape["aux"], mesh.shape["tr"])
    return jax.shard_map(
        functools.partial(body, *sizes), mesh=mesh, in_specs=in_specs, out_specs=out_specs, check_vma=False
    )
```

```python
import contextlib
import functools

import jax
import jax.numpy as jnp
from jax import lax
from jax.experimental import pallas as pl
from jax.experimental.pallas import tpu as pltpu
from jax.sharding import PartitionSpec as P

F32 = jnp.float32
BF16 = jnp.bfloat16
CHUNK = 32
BLEND = 32
LANES = 128
MESH = pl.DeviceIdType.MESH


def scope(name):
    return contextlib.nullcontext()


def kernel(
    naux, ntr,
    live_ref, trial_hbm, val_hbm, cond_hbm, occ_hbm, virt_hbm, pair_hbm,
    out_ref, inter_ref,
    trial_ref, val_ref, cond_ref, occ, virt, pair, blended, acc, mixed, trial_k, own_row,
    block_send, block_recv, cross_recv, mate_recv, proj_send, proj_recv, proj_all, proj_mate,
    sum_send, sum_recv, dots_send, dots_recv, core_recv, final_send, final_recv,
    load_sem, block_sem, proj_sem, sum_sem, dots_sem, extra_ssem, extra_rsem,
):
    g = lax.axis_index("grp")
    a = lax.axis_index("aux")
    t = lax.axis_index("tr")
    own_val, vectors, cond = trial_ref.shape
    half = vectors // 2
    slots, val, _ = occ.shape
    here = a * ntr + t

    arrays = ((trial_hbm, trial_ref), (val_hbm, val_ref), (cond_hbm, cond_ref),
              (pair_hbm, pair), (occ_hbm, occ), (virt_hbm, virt))
    loads = [pltpu.make_async_copy(src, dst, load_sem.at[n]) for n, (src, dst) in enumerate(arrays)]
    pair_copy, occ_copy, virt_copy = loads[3:]
    for copy in loads[:3]:
        copy.start()

    everyone = [(da, dt) for da in range(naux) for dt in range(ntr) if (da, dt) != (0, 0)]

    def peer(da, dt):
        return {"aux": lax.rem(a + da, naux), "tr": lax.rem(t + dt, ntr)}

    def send(src, dst, ssem, rsem, device):
        return pltpu.make_async_remote_copy(
            src_ref=src, dst_ref=dst, send_sem=ssem, recv_sem=rsem, device_id=device, device_id_type=MESH)

    def drain(refs, sem):
        return pltpu.make_async_copy(refs, refs, sem).wait

    mate = {"grp": 1 - g}
    barrier = pltpu.get_barrier_semaphore()
    with scope("signals"):
        for da, dt in everyone:
            pl.semaphore_signal(barrier, inc=1, device_id=peer(da, dt), device_id_type=MESH)
        pl.semaphore_signal(barrier, inc=1, device_id=mate, device_id_type=MESH)
    for copy in loads[3:]:
        copy.start()

    with scope("prep"):
        for copy in loads[:3]:
            copy.wait()
        square = (own_val, own_val)
        diagonal = lax.broadcasted_iota(jnp.int32, square, 0) == lax.broadcasted_iota(jnp.int32, square, 1)
        val_column = jnp.sum(jnp.where(diagonal, val_ref[...], 0.0), axis=1, keepdims=True)
        gap = cond_ref[...] - val_column
        for k in range(vectors):
            trial_k[k] = trial_ref[:, k, :]

    pairs = half * vectors
    lane = lax.broadcasted_iota(jnp.int32, (vectors, LANES), 1)
    vector = lax.broadcasted_iota(jnp.int32, (vectors, LANES), 0)

    def fold(x):
        return sum(x[:, n * LANES:(n + 1) * LANES] for n in range(x.shape[1] // LANES))

    def row_of(parts):
        rows = jnp.concatenate([jnp.sum(p, axis=0, keepdims=True) for part in parts for p in part], axis=0)
        n = lax.broadcasted_iota(jnp.int32, (pairs, LANES), 0)
        j = n // vectors
        place = j * vectors + lax.rem(n - j * vectors + g * half, vectors)
        spread = lax.broadcasted_iota(jnp.int32, (pairs, LANES), 1) == place
        return jnp.sum(jnp.where(spread, jnp.sum(rows, axis=1, keepdims=True), 0.0), axis=0, keepdims=True)

    def column(row, j):
        return jnp.sum(jnp.where(lane == j * vectors + vector, row, 0.0), axis=1, keepdims=True)

    def contract(cols):
        acc[...] = jnp.zeros_like(acc)

        @pl.loop(0, slots // CHUNK)
        def _(i):
            acc[...] += jnp.dot(
                blended[i], virt[pl.ds(i * CHUNK, CHUNK), :, cols].reshape(CHUNK * cond, cond),
                preferred_element_type=F32)

    def apply(it, x):
        finals = []

        def go(copy):
            copy.start()
            finals.append(copy.wait_send)
            return copy

        with scope("pack"):
            block = jnp.concatenate(x, axis=1).astype(BF16)
            block_send[it] = block
            block_recv[it, a] = block
        if it == 0:
            with scope("barrier"):
                pl.semaphore_wait(barrier, len(everyone) + 1)
        with scope("gather_issue"):
            for d in range(1, naux):
                send(block_send.at[it], block_recv.at[it, a], block_sem.at[0, it], block_sem.at[1, it], peer(d, 0)).start()
            blocks = block_recv.at[it, pl.ds(0, naux - 1)]
            finals.append(drain(blocks, block_sem.at[0, it]))

        with scope("project"):
            if it == 0:
                pair_copy.wait()
            for k in range(half):
                mixed[:, k, :] = x[k]
            proj = jnp.zeros((half, pair.shape[2]), F32)
            for v in range(own_val):
                proj += jnp.dot(mixed[v].astype(BF16), pair[v], preferred_element_type=F32)
            proj_send[it] = proj.astype(BF16)
            proj_recv[it, here] = proj.astype(BF16)

        if it == 0:
            with scope("mask"):
                occ_copy.wait()
                live = live_ref[0]
                step = min(16, slots)

                @pl.loop(0, slots // step)
                def _(i):
                    for q in range(step):
                        p = i * step + q
                        keep = jnp.full((val, val), jnp.where(p < live, 1.0, 0.0), F32).astype(BF16)
                        occ[p] = occ[p] * keep

                others = [trial_k[lax.rem(g * half + n, vectors)] for n in range(vectors)]
                own_row[...] = row_of([[fold(gap * others[j] * others[n]) for n in range(vectors)] for j in range(half)])

        with scope("gather_wait"):
            drain(blocks, block_sem.at[1, it])()
        if it == 0:
            mate_cross = send(cross_recv, mate_recv.at[1], extra_ssem.at[2], extra_rsem.at[2], mate)
        with scope("proj_issue"):
            for da, dt in everyone:
                send(proj_send.at[it], proj_recv.at[it, here], proj_sem.at[0, it], proj_sem.at[1, it], peer(da, dt)).start()
            projections = proj_recv.at[it, pl.ds(0, len(everyone))]
            finals.append(drain(projections, proj_sem.at[0, it]))
            if it == 0:
                mate_own = go(send(block_recv.at[0], mate_recv.at[0], extra_ssem.at[0], extra_rsem.at[0], mate))
                cross = go(send(block_recv.at[0], cross_recv, extra_ssem.at[1], extra_rsem.at[1], peer(0, 1)))
        with scope("blend"):
            wide = jnp.concatenate([block_recv[it, s].astype(F32) for s in range(naux)], axis=0).astype(BF16)
            columns = [wide[:, k * cond:(k + 1) * cond] for k in range(half)]

            @pl.loop(0, slots // BLEND)
            def _(i):
                rows = occ[pl.ds(i * BLEND, BLEND)].reshape(BLEND * val, val)
                for k in range(half):
                    b = jnp.dot(rows, columns[k], preferred_element_type=F32).astype(BF16)
                    for q in range(BLEND):
                        blended[i * (BLEND // CHUNK) + q // CHUNK, k * val:(k + 1) * val,
                                (q % CHUNK) * cond:(q % CHUNK + 1) * cond] = b[q * val:(q + 1) * val]

        if it == 0:
            with scope("virt_wait"):
                virt_copy.wait()

        def sum_copies(dt):
            return [
                send(sum_send.at[it, dt, lax.rem(a + d, naux)], sum_recv.at[it, dt * naux + d],
                     sum_sem.at[0, it], sum_sem.at[1, it], peer(d, dt))
                for d in range(1 - dt, naux)]

        with scope("contract"):
            @pl.loop(0, 2)
            def _(j):
                start = pl.multiple_of(lax.rem(t + 1 - j, ntr) * cond, cond)
                contract(pl.ds(start, cond))
                for s in range(naux):
                    for k in range(half):
                        row = k * val + s * own_val
                        sum_send[it, 1 - j, s, :, k * cond:(k + 1) * cond] = acc[row:row + own_val, :].astype(BF16)

                @pl.when(j == 0)
                def _():
                    for copy in sum_copies(1):
                        copy.start()
                    if it == 0:
                        cross.wait_recv()
                        mate_cross.start()

        with scope("sum_issue"):
            for copy in sum_copies(0):
                copy.start()
            sums = sum_recv.at[it, pl.ds(1, len(everyone))]
            finals.append(drain(sums, sum_sem.at[0, it]))
            if it == 0:
                finals.append(mate_cross.wait_send)

        if it == 0:
            with scope("overlap"):
                mate_own.wait_recv()
                mate_cross.wait_recv()
                parts = [[jnp.zeros((own_val, LANES), F32)] * vectors for _ in range(half)]
                for dt in range(2):
                    for s in range(naux):
                        part = sum_send[0, dt, s].astype(F32)
                        same = (block_recv[0, s] if dt == 0 else cross_recv[s]).astype(F32)
                        other = mate_recv[dt, s].astype(F32)
                        both = [y[:, k * cond:(k + 1) * cond] for y in (same, other) for k in range(half)]
                        for j in range(half):
                            mine = part[:, j * cond:(j + 1) * cond]
                            for n in range(vectors):
                                parts[j][n] = parts[j][n] + fold(mine * both[n])
                row = own_row[...] + row_of(parts)
                dots_send[...] = row
                dots_recv[here] = row
            with scope("dots_issue"):
                for da, dt in everyone:
                    send(dots_send, dots_recv.at[here], dots_sem.at[0], dots_sem.at[1], peer(da, dt)).start()

        with scope("exchange"):
            drain(projections, proj_sem.at[1, it])()
            proj = proj_recv[it, 0].astype(F32)
            for n in range(1, naux * ntr):
                proj += proj_recv[it, n].astype(F32)
            if it == 0:
                proj_all[...] = proj
                mate_proj = go(send(proj_all, proj_mate, extra_ssem.at[3], extra_rsem.at[3], mate))
            proj_b = proj.astype(BF16)
            for v in range(own_val):
                mixed[v] = lax.dot_general(
                    proj_b, pair[v], (((1,), (1,)), ((), ())), preferred_element_type=F32)
            local = [gap * x[k] + mixed[:, k, :] for k in range(half)]

        with scope("sum_wait"):
            drain(sums, sum_sem.at[1, it])()
        with scope("combine"):
            total = sum_send[it, 0, a].astype(F32)
            for n in range(1, naux * ntr):
                total += sum_recv[it, n].astype(F32)
            result = [local[k] + total[:, k * cond:(k + 1) * cond] for k in range(half)]
        return result, proj_b, mate_proj if it == 0 else None, finals

    first, proj_b, mate_proj, finals = apply(0, [trial_k[g * half + k] for k in range(half)])

    with scope("dots_wait"):
        mate_proj.wait_recv()
        dots = dots_recv.at[pl.ds(0, len(everyone))]
        drain(dots, dots_sem.at[1])()
        finals.append(drain(dots, dots_sem.at[0]))
    with scope("correct"):
        row = dots_recv[0]
        for n in range(1, naux * ntr):
            row += dots_recv[n]
        both = jnp.concatenate([proj_all[...], proj_mate[...]], axis=0)
        both = jnp.where(g == 0, both, jnp.concatenate([proj_mate[...], proj_all[...]], axis=0))
        inter = []
        for j in range(half):
            exchanged = jnp.sum(fold(both * proj_b[j:j + 1].astype(F32)), axis=1, keepdims=True)
            inter.append((column(row, j) + exchanged) / (naux * own_val * ntr * cond))
        square = jnp.zeros((vectors, LANES), F32)
        for j in range(half):
            square += jnp.where(lane == g * half + j, inter[j], 0.0)
        core_recv[0] = square
        core_dots = send(core_recv.at[0], core_recv.at[1], extra_ssem.at[4], extra_rsem.at[4], mate)
        core_dots.start()

        correction = []
        for j in range(half):
            fitted = trial_k[0] * inter[j][0:1, :]
            for k in range(1, vectors):
                fitted += trial_k[k] * inter[j][k:k + 1, :]
            correction.append((first[j] - fitted) / gap)

    second, _, _, more = apply(1, correction)
    with scope("final_pack"):
        for k in range(half):
            final_send[k] = second[k]
        final_copy = send(final_send, final_recv, extra_ssem.at[5], extra_rsem.at[5], mate)
        final_copy.start()
        for k in range(half):
            out_ref[g * half + k] = second[k]
    with scope("final_sends"):
        core_dots.wait()
        inter_ref[...] = (core_recv[0] + core_recv[1])[:, :vectors]
        for wait in finals + more:
            wait()
    with scope("final_wait"):
        final_copy.wait()
    with scope("final_store"):
        for k in range(half):
            out_ref[(1 - g) * half + k] = final_recv[k]


def finish(applied_ref, inter_ref, out_ref, inter_out_ref):
    for k in range(applied_ref.shape[0]):
        out_ref[:, k, :] = applied_ref[k]
    inter_out_ref[...] = inter_ref[...]


def body(naux, ntr, trial_vectors, energy_val, energy_cond, coef_occ, coef_virt, pair_coef, live_aux):
    own_val, vectors, cond = trial_vectors.shape
    slots, val, _ = coef_occ.shape
    naux_all = pair_coef.shape[2]
    half = vectors // 2
    peers = naux * ntr
    vmem = pl.BlockSpec(memory_space=pltpu.VMEM)
    hbm = pl.BlockSpec(memory_space=pltpu.HBM)
    dma = pltpu.SemaphoreType.DMA
    block = (own_val, half * cond)
    scratch = [
        pltpu.VMEM(trial_vectors.shape, F32),
        pltpu.VMEM((1, own_val), F32),
        pltpu.VMEM((1, cond), F32),
        pltpu.VMEM(coef_occ.shape, BF16),
        pltpu.VMEM(coef_virt.shape, BF16),
        pltpu.VMEM(pair_coef.shape, BF16),
        pltpu.VMEM((slots // CHUNK, half * val, CHUNK * cond), BF16),
        pltpu.VMEM((half * val, cond), F32),
        pltpu.VMEM((own_val, half, cond), F32),
        pltpu.VMEM((vectors, own_val, cond), F32),
        pltpu.VMEM((1, LANES), F32),
        pltpu.VMEM((2, *block), BF16),
        pltpu.VMEM((2, naux, *block), BF16),
        pltpu.VMEM((naux, *block), BF16),
        pltpu.VMEM((2, naux, *block), BF16),
        pltpu.VMEM((2, half, naux_all), BF16),
        pltpu.VMEM((2, peers, half, naux_all), BF16),
        pltpu.VMEM((half, naux_all), F32),
        pltpu.VMEM((half, naux_all), F32),
        pltpu.VMEM((2, ntr, naux, *block), BF16),
        pltpu.VMEM((2, peers, *block), BF16),
        pltpu.VMEM((1, LANES), F32),
        pltpu.VMEM((peers, 1, LANES), F32),
        pltpu.VMEM((2, vectors, LANES), F32),
        pltpu.VMEM((half, own_val, cond), F32),
        pltpu.VMEM((half, own_val, cond), F32),
        dma((6,)),
        dma((2, 2)),
        dma((2, 2)),
        dma((2, 2)),
        dma((2,)),
        dma((6,)),
        dma((6,)),
    ]
    applied, intersection = pl.pallas_call(
        functools.partial(kernel, naux, ntr),
        out_shape=(
            jax.ShapeDtypeStruct((vectors, own_val, cond), F32),
            jax.ShapeDtypeStruct((vectors, vectors), F32),
        ),
        in_specs=[pl.BlockSpec(memory_space=pltpu.SMEM)] + [hbm] * 6,
        out_specs=(vmem, vmem),
        scratch_shapes=scratch,
        compiler_params=pltpu.CompilerParams(
            collective_id=0, has_side_effects=True, vmem_limit_bytes=40 * 1024 * 1024
        ),
    )(
        live_aux, *[pltpu.with_memory_space_constraint(x, pltpu.HBM) for x in (
            trial_vectors, energy_val.reshape(1, -1), energy_cond.reshape(1, -1), coef_occ, coef_virt, pair_coef)]
    )
    return pl.pallas_call(
        finish,
        out_shape=(
            jax.ShapeDtypeStruct(trial_vectors.shape, F32),
            jax.ShapeDtypeStruct((vectors, vectors), F32),
        ),
        in_specs=[vmem, vmem],
        out_specs=(vmem, vmem),
        compiler_params=pltpu.CompilerParams(vmem_limit_bytes=2 * 1024 * 1024),
    )(applied, intersection)


def solution(mesh):
    in_specs = (
        P("aux", None, "tr"),
        P("aux"),
        P("tr"),
        P("aux", None, None),
        P("aux", "tr", None),
        P("aux", "tr", None),
        P("aux"),
    )
    out_specs = (P("aux", None, "tr"), P())
    sizes = (mesh.shape["aux"], mesh.shape["tr"])
    return jax.shard_map(
        functools.partial(body, *sizes), mesh=mesh, in_specs=in_specs, out_specs=out_specs, check_vma=False
    )
```

```python
import contextlib
import functools

import jax
import jax.numpy as jnp
from jax import lax
from jax.experimental import pallas as pl
from jax.experimental.pallas import tpu as pltpu
from jax.sharding import PartitionSpec as P

F32 = jnp.float32
BF16 = jnp.bfloat16
BLEND = 32
LANES = 128
MESH = pl.DeviceIdType.MESH


def scope(name):
    return contextlib.nullcontext()


def kernel(
    naux, ntr,
    live_ref, trial_hbm, val_hbm, cond_hbm, occ_hbm, virt_hbm, pair_hbm,
    out_ref, inter_ref,
    trial_ref, val_ref, cond_ref, occ, virt, pair, blended, acc, mixed, trial_k, own_row,
    block_send, block_recv, cross_recv, mate_recv, proj_send, proj_recv, proj_all, proj_mate,
    sum_send, sum_recv, dots_send, dots_recv, core_recv, final_send, final_recv,
    load_sem, block_sem, proj_sem, sum_sem, dots_sem, extra_ssem, extra_rsem,
):
    g = lax.axis_index("grp")
    a = lax.axis_index("aux")
    t = lax.axis_index("tr")
    own_val, vectors, cond = trial_ref.shape
    half = vectors // 2
    size = half // 2
    slots, val, _ = occ.shape
    here = a * ntr + t

    arrays = ((trial_hbm, trial_ref), (val_hbm, val_ref), (cond_hbm, cond_ref),
              (pair_hbm, pair), (occ_hbm, occ), (virt_hbm, virt))
    loads = [pltpu.make_async_copy(src, dst, load_sem.at[n]) for n, (src, dst) in enumerate(arrays)]
    pair_copy, occ_copy, virt_copy = loads[3:]
    for copy in loads[:3]:
        copy.start()

    everyone = [(da, dt) for da in reversed(range(naux)) for dt in reversed(range(ntr)) if (da, dt) != (0, 0)]

    def along(d):
        if naux & (naux - 1):
            return lax.rem(a + d, naux)
        bits = [1 << i for i in range(naux.bit_length()) if d >> i & 1]
        return a + sum(bit * (1 - 2 * (a // bit % 2)) for bit in bits)

    def peer(da, dt):
        return {"aux": along(da), "tr": lax.rem(t + dt, ntr)}

    def send(src, dst, ssem, rsem, device):
        return pltpu.make_async_remote_copy(
            src_ref=src, dst_ref=dst, send_sem=ssem, recv_sem=rsem, device_id=device, device_id_type=MESH)

    def drain(refs, sem):
        return pltpu.make_async_copy(refs, refs, sem).wait

    mate = {"grp": 1 - g}
    barrier = pltpu.get_barrier_semaphore()
    with scope("signals"):
        greeted = [peer(da, 0) for da in reversed(range(1, naux))] + [peer(0, dt) for dt in range(1, ntr)] + [mate]
        for device in greeted:
            pl.semaphore_signal(barrier, inc=1, device_id=device, device_id_type=MESH)
    for copy in loads[3:]:
        copy.start()

    with scope("prep"):
        for copy in loads[:3]:
            copy.wait()
        square = (own_val, own_val)
        diagonal = lax.broadcasted_iota(jnp.int32, square, 0) == lax.broadcasted_iota(jnp.int32, square, 1)
        val_column = jnp.sum(jnp.where(diagonal, val_ref[...], 0.0), axis=1, keepdims=True)
        gap = cond_ref[...] - val_column
        for k in range(vectors):
            trial_k[k] = trial_ref[:, k, :]

    pairs = half * vectors
    lane = lax.broadcasted_iota(jnp.int32, (vectors, LANES), 1)
    vector = lax.broadcasted_iota(jnp.int32, (vectors, LANES), 0)

    def fold(x):
        return sum(x[:, n * LANES:(n + 1) * LANES] for n in range(x.shape[1] // LANES))

    def row_of(parts):
        rows = jnp.concatenate([jnp.sum(p, axis=0, keepdims=True) for part in parts for p in part], axis=0)
        n = lax.broadcasted_iota(jnp.int32, (pairs, LANES), 0)
        j = n // vectors
        place = j * vectors + lax.rem(n - j * vectors + g * half, vectors)
        spread = lax.broadcasted_iota(jnp.int32, (pairs, LANES), 1) == place
        return jnp.sum(jnp.where(spread, jnp.sum(rows, axis=1, keepdims=True), 0.0), axis=0, keepdims=True)

    def column(row, j):
        return jnp.sum(jnp.where(lane == j * vectors + vector, row, 0.0), axis=1, keepdims=True)

    def apply(it, x):
        finals = []

        def go(copy):
            copy.start()
            finals.append(copy.wait_send)
            return copy

        with scope("pack"):
            for h in range(2):
                block = jnp.concatenate(x[h * size:(h + 1) * size], axis=1).astype(BF16)
                block_send[it, h] = block
                block_recv[it, h, a] = block
        if it == 0:
            with scope("barrier"):
                pl.semaphore_wait(barrier, len(greeted))
        with scope("gather_issue"):
            for h in range(2):
                for d in reversed(range(1, naux)):
                    send(block_send.at[it, h], block_recv.at[it, h, a],
                         block_sem.at[0, it, h], block_sem.at[1, it, h], peer(d, 0)).start()
                blocks = block_recv.at[it, h, pl.ds(0, naux - 1)]
                finals.append(drain(blocks, block_sem.at[0, it, h]))

        with scope("project"):
            if it == 0:
                pair_copy.wait()
            for k in range(half):
                mixed[:, k, :] = x[k]
            proj = jnp.zeros((half, pair.shape[2]), F32)
            for v in range(own_val):
                proj += jnp.dot(mixed[v].astype(BF16), pair[v], preferred_element_type=F32)
            proj_send[it] = proj.astype(BF16)
            proj_recv[it, here] = proj.astype(BF16)

        if it == 0:
            with scope("mask"):
                occ_copy.wait()
                live = live_ref[0]
                step = min(16, slots)

                @pl.loop(0, slots // step)
                def _(i):
                    for q in range(step):
                        p = i * step + q
                        keep = jnp.full((val, val), jnp.where(p < live, 1.0, 0.0), F32).astype(BF16)
                        occ[p] = occ[p] * keep

                others = [trial_k[lax.rem(g * half + n, vectors)] for n in range(vectors)]
                own_row[...] = row_of([[fold(gap * others[j] * others[n]) for n in range(vectors)] for j in range(half)])

        crosses, mates = [], []
        mate_cross = send(cross_recv, mate_recv.at[1], extra_ssem.at[4], extra_rsem.at[4], mate)
        for h in range(2):
            with scope("gather_wait"):
                drain(block_recv.at[it, h, pl.ds(0, naux - 1)], block_sem.at[1, it, h])()
            if it == 0:
                crosses.append(go(send(
                    block_recv.at[0, h], cross_recv.at[h], extra_ssem.at[h], extra_rsem.at[h], peer(0, 1))))
                mates.append(go(send(
                    block_recv.at[0, h], mate_recv.at[0, h], extra_ssem.at[2 + h], extra_rsem.at[2 + h], mate)))
            if h == 1:
                with scope("proj_issue"):
                    for da, dt in everyone:
                        send(proj_send.at[it], proj_recv.at[it, here], proj_sem.at[0, it], proj_sem.at[1, it],
                             peer(da, dt)).start()
                    projections = proj_recv.at[it, pl.ds(0, len(everyone))]
                    finals.append(drain(projections, proj_sem.at[0, it]))
            with scope("blend"):
                wide = jnp.concatenate([block_recv[it, h, s].astype(F32) for s in range(naux)], axis=0).astype(BF16)
                columns = [wide[:, k * cond:(k + 1) * cond] for k in range(size)]

                @pl.loop(0, slots // BLEND)
                def _(i):
                    rows = occ[pl.ds(i * BLEND, BLEND)].reshape(BLEND * val, val)
                    for k in range(size):
                        b = jnp.dot(rows, columns[k], preferred_element_type=F32).astype(BF16)
                        for q in range(BLEND):
                            blended[i, (h * size + k) * val:(h * size + k + 1) * val,
                                    q * cond:(q + 1) * cond] = b[q * val:(q + 1) * val]

        if it == 0:
            with scope("virt_wait"):
                virt_copy.wait()

        def contract(rows, dt):
            start = pl.multiple_of(lax.rem(t + dt, ntr) * cond, cond)
            mixture = jnp.concatenate([blended[i, rows, :] for i in range(slots // BLEND)], axis=1)
            acc[:rows.size] = jnp.dot(
                mixture, virt[:, :, pl.ds(start, cond)].reshape(slots * cond, cond), preferred_element_type=F32)

        def pack(dt, h, base):
            for s in range(naux):
                for k in range(size):
                    row = base + k * val + s * own_val
                    sum_send[it, dt, h, s, :, k * cond:(k + 1) * cond] = acc[row:row + own_val, :].astype(BF16)

        def post(dt, h):
            for d in reversed(range(1 - dt, naux)):
                send(sum_send.at[it, dt, h, along(d)], sum_recv.at[it, (dt * naux + d) * 2 + h],
                     sum_sem.at[0, it], sum_sem.at[1, it], peer(d, dt)).start()

        with scope("contract_a"):
            contract(pl.ds(0, half * val), 1)
            for h in range(2):
                pack(1, h, h * size * val)
                post(1, h)
        with scope("contract_b"):
            @pl.loop(0, 2)
            def _(h):
                contract(pl.ds(pl.multiple_of(h * size * val, size * val), size * val), 0)
                pack(0, h, 0)
                post(0, h)
                if it == 0:
                    @pl.when(h == 0)
                    def _():
                        for copy in crosses:
                            copy.wait_recv()
                        mate_cross.start()

        with scope("sum_issue"):
            sums = sum_recv.at[it, pl.ds(2, 2 * len(everyone))]
            finals.append(drain(sums, sum_sem.at[0, it]))
            if it == 0:
                finals.append(mate_cross.wait_send)

        if it == 0:
            with scope("overlap"):
                for copy in mates:
                    copy.wait_recv()
                mate_cross.wait_recv()
                parts = [[jnp.zeros((own_val, LANES), F32)] * vectors for _ in range(half)]
                for dt in range(2):
                    for s in range(naux):
                        same = block_recv.at[0] if dt == 0 else cross_recv
                        both = [
                            ref[h, s, :, k * cond:(k + 1) * cond].astype(F32)
                            for ref in (same, mate_recv.at[dt]) for h in range(2) for k in range(size)]
                        for j in range(half):
                            where = pl.ds(j % size * cond, cond)
                            mine = sum_send[0, dt, j // size, s, :, where].astype(F32)
                            for n in range(vectors):
                                parts[j][n] = parts[j][n] + fold(mine * both[n])
                row = own_row[...] + row_of(parts)
                dots_send[...] = row
                dots_recv[here] = row
            with scope("dots_issue"):
                for da, dt in everyone:
                    send(dots_send, dots_recv.at[here], dots_sem.at[0], dots_sem.at[1], peer(da, dt)).start()

        with scope("exchange"):
            drain(projections, proj_sem.at[1, it])()
            proj = proj_recv[it, 0].astype(F32)
            for n in range(1, naux * ntr):
                proj += proj_recv[it, n].astype(F32)
            if it == 0:
                proj_all[...] = proj
                mate_proj = go(send(proj_all, proj_mate, extra_ssem.at[5], extra_rsem.at[5], mate))
            proj_b = proj.astype(BF16)
            for v in range(own_val):
                mixed[v] = lax.dot_general(
                    proj_b, pair[v], (((1,), (1,)), ((), ())), preferred_element_type=F32)
            local = [gap * x[k] + mixed[:, k, :] for k in range(half)]

        with scope("sum_wait"):
            drain(sums, sum_sem.at[1, it])()
        with scope("combine"):
            result = []
            for h in range(2):
                total = sum_send[it, 0, h, a].astype(F32)
                for n in range(1, naux * ntr):
                    total += sum_recv[it, n * 2 + h].astype(F32)
                result += [local[h * size + k] + total[:, k * cond:(k + 1) * cond] for k in range(size)]
        return result, proj_b, mate_proj if it == 0 else None, finals

    first, proj_b, mate_proj, finals = apply(0, [trial_k[g * half + k] for k in range(half)])

    with scope("dots_wait"):
        mate_proj.wait_recv()
        dots = dots_recv.at[pl.ds(0, len(everyone))]
        drain(dots, dots_sem.at[1])()
        finals.append(drain(dots, dots_sem.at[0]))
    with scope("correct"):
        row = dots_recv[0]
        for n in range(1, naux * ntr):
            row += dots_recv[n]
        both = jnp.concatenate([proj_all[...], proj_mate[...]], axis=0)
        both = jnp.where(g == 0, both, jnp.concatenate([proj_mate[...], proj_all[...]], axis=0))
        inter = []
        for j in range(half):
            exchanged = jnp.sum(fold(both * proj_b[j:j + 1].astype(F32)), axis=1, keepdims=True)
            inter.append((column(row, j) + exchanged) / (naux * own_val * ntr * cond))
        square = jnp.zeros((vectors, LANES), F32)
        for j in range(half):
            square += jnp.where(lane == g * half + j, inter[j], 0.0)
        core_recv[0] = square
        core_dots = send(core_recv.at[0], core_recv.at[1], extra_ssem.at[6], extra_rsem.at[6], mate)
        core_dots.start()

        correction = []
        for j in range(half):
            fitted = trial_k[0] * inter[j][0:1, :]
            for k in range(1, vectors):
                fitted += trial_k[k] * inter[j][k:k + 1, :]
            correction.append((first[j] - fitted) / gap)

    second, _, _, more = apply(1, correction)
    with scope("final_pack"):
        for k in range(half):
            final_send[k] = second[k]
        final_copy = send(final_send, final_recv, extra_ssem.at[7], extra_rsem.at[7], mate)
        final_copy.start()
        for k in range(half):
            out_ref[g * half + k] = second[k]
    with scope("final_sends"):
        core_dots.wait()
        inter_ref[...] = (core_recv[0] + core_recv[1])[:, :vectors]
        for wait in finals + more:
            wait()
    with scope("final_wait"):
        final_copy.wait()
    with scope("final_store"):
        for k in range(half):
            out_ref[(1 - g) * half + k] = final_recv[k]


def finish(applied_ref, inter_ref, out_ref, inter_out_ref):
    for k in range(applied_ref.shape[0]):
        out_ref[:, k, :] = applied_ref[k]
    inter_out_ref[...] = inter_ref[...]


def body(naux, ntr, trial_vectors, energy_val, energy_cond, coef_occ, coef_virt, pair_coef, live_aux):
    own_val, vectors, cond = trial_vectors.shape
    slots, val, _ = coef_occ.shape
    naux_all = pair_coef.shape[2]
    half = vectors // 2
    peers = naux * ntr
    vmem = pl.BlockSpec(memory_space=pltpu.VMEM)
    hbm = pl.BlockSpec(memory_space=pltpu.HBM)
    dma = pltpu.SemaphoreType.DMA
    block = (own_val, half // 2 * cond)
    scratch = [
        pltpu.VMEM(trial_vectors.shape, F32),
        pltpu.VMEM((1, own_val), F32),
        pltpu.VMEM((1, cond), F32),
        pltpu.VMEM(coef_occ.shape, BF16),
        pltpu.VMEM(coef_virt.shape, BF16),
        pltpu.VMEM(pair_coef.shape, BF16),
        pltpu.VMEM((slots // BLEND, half * val, BLEND * cond), BF16),
        pltpu.VMEM((half * val, cond), F32),
        pltpu.VMEM((own_val, half, cond), F32),
        pltpu.VMEM((vectors, own_val, cond), F32),
        pltpu.VMEM((1, LANES), F32),
        pltpu.VMEM((2, 2, *block), BF16),
        pltpu.VMEM((2, 2, naux, *block), BF16),
        pltpu.VMEM((2, naux, *block), BF16),
        pltpu.VMEM((2, 2, naux, *block), BF16),
        pltpu.VMEM((2, half, naux_all), BF16),
        pltpu.VMEM((2, peers, half, naux_all), BF16),
        pltpu.VMEM((half, naux_all), F32),
        pltpu.VMEM((half, naux_all), F32),
        pltpu.VMEM((2, ntr, 2, naux, *block), BF16),
        pltpu.VMEM((2, 2 * peers, *block), BF16),
        pltpu.VMEM((1, LANES), F32),
        pltpu.VMEM((peers, 1, LANES), F32),
        pltpu.VMEM((2, vectors, LANES), F32),
        pltpu.VMEM((half, own_val, cond), F32),
        pltpu.VMEM((half, own_val, cond), F32),
        dma((6,)),
        dma((2, 2, 2)),
        dma((2, 2)),
        dma((2, 2)),
        dma((2,)),
        dma((8,)),
        dma((8,)),
    ]
    applied, intersection = pl.pallas_call(
        functools.partial(kernel, naux, ntr),
        out_shape=(
            jax.ShapeDtypeStruct((vectors, own_val, cond), F32),
            jax.ShapeDtypeStruct((vectors, vectors), F32),
        ),
        in_specs=[pl.BlockSpec(memory_space=pltpu.SMEM)] + [hbm] * 6,
        out_specs=(vmem, vmem),
        scratch_shapes=scratch,
        compiler_params=pltpu.CompilerParams(
            collective_id=0, has_side_effects=True, vmem_limit_bytes=48 * 1024 * 1024
        ),
    )(
        live_aux, *[pltpu.with_memory_space_constraint(x, pltpu.HBM) for x in (
            trial_vectors, energy_val.reshape(1, -1), energy_cond.reshape(1, -1), coef_occ, coef_virt, pair_coef)]
    )
    return pl.pallas_call(
        finish,
        out_shape=(
            jax.ShapeDtypeStruct(trial_vectors.shape, F32),
            jax.ShapeDtypeStruct((vectors, vectors), F32),
        ),
        in_specs=[vmem, vmem],
        out_specs=(vmem, vmem),
        compiler_params=pltpu.CompilerParams(vmem_limit_bytes=2 * 1024 * 1024),
    )(applied, intersection)


def solution(mesh):
    in_specs = (
        P("aux", None, "tr"),
        P("aux"),
        P("tr"),
        P("aux", None, None),
        P("aux", "tr", None),
        P("aux", "tr", None),
        P("aux"),
    )
    out_specs = (P("aux", None, "tr"), P())
    sizes = (mesh.shape["aux"], mesh.shape["tr"])
    return jax.shard_map(
        functools.partial(body, *sizes), mesh=mesh, in_specs=in_specs, out_specs=out_specs, check_vma=False
    )
```

```python
import contextlib
import functools

import jax
import jax.numpy as jnp
from jax import lax
from jax.experimental import pallas as pl
from jax.experimental.pallas import tpu as pltpu
from jax.sharding import PartitionSpec as P

F32 = jnp.float32
BF16 = jnp.bfloat16
BLEND = 64
LANES = 128
MESH = pl.DeviceIdType.MESH


def scope(name):
    return contextlib.nullcontext()


def kernel(
    naux, ntr,
    live_ref, trial_hbm, val_hbm, cond_hbm, occ_hbm, virt_hbm, pair_hbm,
    out_ref, inter_ref,
    trial_ref, val_ref, cond_ref, occ, virt, pair, blended, acc, mixed, trial_k, own_row,
    block_send, block_recv, cross_recv, mate_recv, proj_send, proj_recv, proj_all, proj_mate,
    sum_send, sum_recv, dots_send, dots_recv, core_recv, final_send, final_recv,
    load_sem, block_sem, proj_sem, sum_sem, dots_sem, extra_ssem, extra_rsem,
):
    g = lax.axis_index("grp")
    a = lax.axis_index("aux")
    t = lax.axis_index("tr")
    own_val, vectors, cond = trial_ref.shape
    half = vectors // 2
    size = half // 2
    slots, val, _ = occ.shape
    here = a * ntr + t

    arrays = ((trial_hbm, trial_ref), (val_hbm, val_ref), (cond_hbm, cond_ref),
              (pair_hbm, pair), (occ_hbm, occ), (virt_hbm, virt))
    loads = [pltpu.make_async_copy(src, dst, load_sem.at[n]) for n, (src, dst) in enumerate(arrays)]
    pair_copy, occ_copy, virt_copy = loads[3:]
    for copy in loads[:3]:
        copy.start()

    everyone = [(da, dt) for da in reversed(range(naux)) for dt in reversed(range(ntr)) if (da, dt) != (0, 0)]

    def along(d):
        if naux & (naux - 1):
            return lax.rem(a + d, naux)
        bits = [1 << i for i in range(naux.bit_length()) if d >> i & 1]
        return a + sum(bit * (1 - 2 * (a // bit % 2)) for bit in bits)

    def peer(da, dt):
        return {"aux": along(da), "tr": lax.rem(t + dt, ntr)}

    def send(src, dst, ssem, rsem, device):
        return pltpu.make_async_remote_copy(
            src_ref=src, dst_ref=dst, send_sem=ssem, recv_sem=rsem, device_id=device, device_id_type=MESH)

    def drain(refs, sem):
        return pltpu.make_async_copy(refs, refs, sem).wait

    mate = {"grp": 1 - g}
    barrier = pltpu.get_barrier_semaphore()
    with scope("signals"):
        greeted = [peer(da, 0) for da in reversed(range(1, naux))] + [peer(0, dt) for dt in range(1, ntr)] + [mate]
        for device in greeted:
            pl.semaphore_signal(barrier, inc=1, device_id=device, device_id_type=MESH)
    for copy in loads[3:]:
        copy.start()

    with scope("prep"):
        for copy in loads[:3]:
            copy.wait()
        square = (own_val, own_val)
        diagonal = lax.broadcasted_iota(jnp.int32, square, 0) == lax.broadcasted_iota(jnp.int32, square, 1)
        val_column = jnp.sum(jnp.where(diagonal, val_ref[...], 0.0), axis=1, keepdims=True)
        gap = cond_ref[...] - val_column
        for k in range(vectors):
            trial_k[k] = trial_ref[:, k, :]

    pairs = half * vectors
    lane = lax.broadcasted_iota(jnp.int32, (vectors, LANES), 1)
    vector = lax.broadcasted_iota(jnp.int32, (vectors, LANES), 0)

    def fold(x):
        return sum(x[:, n * LANES:(n + 1) * LANES] for n in range(x.shape[1] // LANES))

    def row_of(parts):
        rows = jnp.concatenate([jnp.sum(p, axis=0, keepdims=True) for part in parts for p in part], axis=0)
        n = lax.broadcasted_iota(jnp.int32, (pairs, LANES), 0)
        j = n // vectors
        place = j * vectors + lax.rem(n - j * vectors + g * half, vectors)
        spread = lax.broadcasted_iota(jnp.int32, (pairs, LANES), 1) == place
        return jnp.sum(jnp.where(spread, jnp.sum(rows, axis=1, keepdims=True), 0.0), axis=0, keepdims=True)

    def column(row, j):
        return jnp.sum(jnp.where(lane == j * vectors + vector, row, 0.0), axis=1, keepdims=True)

    def apply(it, x):
        finals = []

        def go(copy):
            copy.start()
            finals.append(copy.wait_send)
            return copy

        with scope("pack"):
            for h in range(2):
                block = jnp.concatenate(x[h * size:(h + 1) * size], axis=1).astype(BF16)
                block_send[it, h] = block
                block_recv[it, h, a] = block
        if it == 0:
            with scope("barrier"):
                pl.semaphore_wait(barrier, len(greeted))
        with scope("gather_issue"):
            for h in range(2):
                for d in reversed(range(1, naux)):
                    send(block_send.at[it, h], block_recv.at[it, h, a],
                         block_sem.at[0, it, h], block_sem.at[1, it, h], peer(d, 0)).start()
                blocks = block_recv.at[it, h, pl.ds(0, naux - 1)]
                finals.append(drain(blocks, block_sem.at[0, it, h]))

        with scope("project"):
            if it == 0:
                pair_copy.wait()
            for k in range(half):
                mixed[:, k, :] = x[k]
            proj = jnp.zeros((half, pair.shape[2]), F32)
            for v in range(own_val):
                proj += jnp.dot(mixed[v].astype(BF16), pair[v], preferred_element_type=F32)
            proj_send[it] = proj.astype(BF16)
            proj_recv[it, here] = proj.astype(BF16)

        if it == 0:
            with scope("mask"):
                occ_copy.wait()
                live = live_ref[0]
                step = min(16, slots)

                @pl.loop(0, slots // step)
                def _(i):
                    for q in range(step):
                        p = i * step + q
                        keep = jnp.full((val, val), jnp.where(p < live, 1.0, 0.0), F32).astype(BF16)
                        occ[p] = occ[p] * keep

                others = [trial_k[lax.rem(g * half + n, vectors)] for n in range(vectors)]
                own_row[...] = row_of([[fold(gap * others[j] * others[n]) for n in range(vectors)] for j in range(half)])

        crosses, mates = [], []
        mate_cross = send(cross_recv, mate_recv.at[1], extra_ssem.at[4], extra_rsem.at[4], mate)
        for h in range(2):
            with scope("gather_wait"):
                drain(block_recv.at[it, h, pl.ds(0, naux - 1)], block_sem.at[1, it, h])()
            if it == 0:
                crosses.append(go(send(
                    block_recv.at[0, h], cross_recv.at[h], extra_ssem.at[h], extra_rsem.at[h], peer(0, 1))))
                mates.append(go(send(
                    block_recv.at[0, h], mate_recv.at[0, h], extra_ssem.at[2 + h], extra_rsem.at[2 + h], mate)))
            if h == 1:
                with scope("proj_issue"):
                    for da, dt in everyone:
                        send(proj_send.at[it], proj_recv.at[it, here], proj_sem.at[0, it], proj_sem.at[1, it],
                             peer(da, dt)).start()
                    projections = proj_recv.at[it, pl.ds(0, len(everyone))]
                    finals.append(drain(projections, proj_sem.at[0, it]))
            with scope("blend"):
                wide = jnp.concatenate([block_recv[it, h, s].astype(F32) for s in range(naux)], axis=0).astype(BF16)
                columns = [wide[:, k * cond:(k + 1) * cond] for k in range(size)]

                @pl.when(t >= 0)
                def _():
                    i = 0
                    rows = occ[pl.ds(i * BLEND, BLEND)].reshape(BLEND * val, val)
                    for k in range(size):
                        b = jnp.dot(rows, columns[k], preferred_element_type=F32).astype(BF16)
                        for q in range(BLEND):
                            blended[i, (h * size + k) * val:(h * size + k + 1) * val,
                                    q * cond:(q + 1) * cond] = b[q * val:(q + 1) * val]

        if it == 0:
            with scope("virt_wait"):
                virt_copy.wait()

        def contract(rows, dt):
            start = pl.multiple_of(lax.rem(t + dt, ntr) * cond, cond)
            mixture = jnp.concatenate([blended[i, rows, :] for i in range(slots // BLEND)], axis=1)
            acc[:rows.size] = jnp.dot(
                mixture, virt[:, :, pl.ds(start, cond)].reshape(slots * cond, cond), preferred_element_type=F32)

        def pack(dt, h, base):
            for s in range(naux):
                for k in range(size):
                    row = base + k * val + s * own_val
                    sum_send[it, dt, h, s, :, k * cond:(k + 1) * cond] = acc[row:row + own_val, :].astype(BF16)

        def post(dt, h):
            for d in reversed(range(1 - dt, naux)):
                send(sum_send.at[it, dt, h, along(d)], sum_recv.at[it, (dt * naux + d) * 2 + h],
                     sum_sem.at[0, it], sum_sem.at[1, it], peer(d, dt)).start()

        with scope("contract_a"):
            contract(pl.ds(0, half * val), 1)
            for h in range(2):
                pack(1, h, h * size * val)
                post(1, h)
        with scope("contract_b"):
            @pl.loop(0, 2)
            def _(h):
                contract(pl.ds(pl.multiple_of(h * size * val, size * val), size * val), 0)
                pack(0, h, 0)
                post(0, h)
                if it == 0:
                    @pl.when(h == 0)
                    def _():
                        for copy in crosses:
                            copy.wait_recv()
                        mate_cross.start()

        with scope("sum_issue"):
            sums = sum_recv.at[it, pl.ds(2, 2 * len(everyone))]
            finals.append(drain(sums, sum_sem.at[0, it]))
            if it == 0:
                finals.append(mate_cross.wait_send)

        if it == 0:
            with scope("overlap"):
                for copy in mates:
                    copy.wait_recv()
                mate_cross.wait_recv()
                parts = [[jnp.zeros((own_val, LANES), F32)] * vectors for _ in range(half)]
                for dt in range(2):
                    for s in range(naux):
                        same = block_recv.at[0] if dt == 0 else cross_recv
                        both = [
                            ref[h, s, :, k * cond:(k + 1) * cond].astype(F32)
                            for ref in (same, mate_recv.at[dt]) for h in range(2) for k in range(size)]
                        for j in range(half):
                            where = pl.ds(j % size * cond, cond)
                            mine = sum_send[0, dt, j // size, s, :, where].astype(F32)
                            for n in range(vectors):
                                parts[j][n] = parts[j][n] + fold(mine * both[n])
                row = own_row[...] + row_of(parts)
                dots_send[...] = row
                dots_recv[here] = row
            with scope("dots_issue"):
                for da, dt in everyone:
                    send(dots_send, dots_recv.at[here], dots_sem.at[0], dots_sem.at[1], peer(da, dt)).start()

        with scope("exchange"):
            drain(projections, proj_sem.at[1, it])()
            proj = proj_recv[it, 0].astype(F32)
            for n in range(1, naux * ntr):
                proj += proj_recv[it, n].astype(F32)
            if it == 0:
                proj_all[...] = proj
                mate_proj = go(send(proj_all, proj_mate, extra_ssem.at[5], extra_rsem.at[5], mate))
            proj_b = proj.astype(BF16)
            for v in range(own_val):
                mixed[v] = lax.dot_general(
                    proj_b, pair[v], (((1,), (1,)), ((), ())), preferred_element_type=F32)
            local = [gap * x[k] + mixed[:, k, :] for k in range(half)]

        with scope("sum_wait"):
            drain(sums, sum_sem.at[1, it])()
        with scope("combine"):
            result = []
            for h in range(2):
                total = sum_send[it, 0, h, a].astype(F32)
                for n in range(1, naux * ntr):
                    total += sum_recv[it, n * 2 + h].astype(F32)
                result += [local[h * size + k] + total[:, k * cond:(k + 1) * cond] for k in range(size)]
        return result, proj_b, mate_proj if it == 0 else None, finals

    first, proj_b, mate_proj, finals = apply(0, [trial_k[g * half + k] for k in range(half)])

    with scope("dots_wait"):
        mate_proj.wait_recv()
        dots = dots_recv.at[pl.ds(0, len(everyone))]
        drain(dots, dots_sem.at[1])()
        finals.append(drain(dots, dots_sem.at[0]))
    with scope("correct"):
        row = dots_recv[0]
        for n in range(1, naux * ntr):
            row += dots_recv[n]
        both = jnp.concatenate([proj_all[...], proj_mate[...]], axis=0)
        both = jnp.where(g == 0, both, jnp.concatenate([proj_mate[...], proj_all[...]], axis=0))
        inter = []
        for j in range(half):
            exchanged = jnp.sum(fold(both * proj_b[j:j + 1].astype(F32)), axis=1, keepdims=True)
            inter.append((column(row, j) + exchanged) / (naux * own_val * ntr * cond))
        square = jnp.zeros((vectors, LANES), F32)
        for j in range(half):
            square += jnp.where(lane == g * half + j, inter[j], 0.0)
        core_recv[0] = square
        core_dots = send(core_recv.at[0], core_recv.at[1], extra_ssem.at[6], extra_rsem.at[6], mate)
        core_dots.start()

        correction = []
        for j in range(half):
            fitted = trial_k[0] * inter[j][0:1, :]
            for k in range(1, vectors):
                fitted += trial_k[k] * inter[j][k:k + 1, :]
            correction.append((first[j] - fitted) / gap)

    second, _, _, more = apply(1, correction)
    with scope("final_pack"):
        for k in range(half):
            final_send[k] = second[k]
        final_copy = send(final_send, final_recv, extra_ssem.at[7], extra_rsem.at[7], mate)
        final_copy.start()
        for k in range(half):
            out_ref[g * half + k] = second[k]
    with scope("final_sends"):
        core_dots.wait()
        inter_ref[...] = (core_recv[0] + core_recv[1])[:, :vectors]
        for wait in finals + more:
            wait()
    with scope("final_wait"):
        final_copy.wait()
    with scope("final_store"):
        for k in range(half):
            out_ref[(1 - g) * half + k] = final_recv[k]


def finish(applied_ref, inter_ref, out_ref, inter_out_ref):
    for k in range(applied_ref.shape[0]):
        out_ref[:, k, :] = applied_ref[k]
    inter_out_ref[...] = inter_ref[...]


def body(naux, ntr, trial_vectors, energy_val, energy_cond, coef_occ, coef_virt, pair_coef, live_aux):
    own_val, vectors, cond = trial_vectors.shape
    slots, val, _ = coef_occ.shape
    naux_all = pair_coef.shape[2]
    half = vectors // 2
    peers = naux * ntr
    vmem = pl.BlockSpec(memory_space=pltpu.VMEM)
    hbm = pl.BlockSpec(memory_space=pltpu.HBM)
    dma = pltpu.SemaphoreType.DMA
    block = (own_val, half // 2 * cond)
    scratch = [
        pltpu.VMEM(trial_vectors.shape, F32),
        pltpu.VMEM((1, own_val), F32),
        pltpu.VMEM((1, cond), F32),
        pltpu.VMEM(coef_occ.shape, BF16),
        pltpu.VMEM(coef_virt.shape, BF16),
        pltpu.VMEM(pair_coef.shape, BF16),
        pltpu.VMEM((slots // BLEND, half * val, BLEND * cond), BF16),
        pltpu.VMEM((half * val, cond), F32),
        pltpu.VMEM((own_val, half, cond), F32),
        pltpu.VMEM((vectors, own_val, cond), F32),
        pltpu.VMEM((1, LANES), F32),
        pltpu.VMEM((2, 2, *block), BF16),
        pltpu.VMEM((2, 2, naux, *block), BF16),
        pltpu.VMEM((2, naux, *block), BF16),
        pltpu.VMEM((2, 2, naux, *block), BF16),
        pltpu.VMEM((2, half, naux_all), BF16),
        pltpu.VMEM((2, peers, half, naux_all), BF16),
        pltpu.VMEM((half, naux_all), F32),
        pltpu.VMEM((half, naux_all), F32),
        pltpu.VMEM((2, ntr, 2, naux, *block), BF16),
        pltpu.VMEM((2, 2 * peers, *block), BF16),
        pltpu.VMEM((1, LANES), F32),
        pltpu.VMEM((peers, 1, LANES), F32),
        pltpu.VMEM((2, vectors, LANES), F32),
        pltpu.VMEM((half, own_val, cond), F32),
        pltpu.VMEM((half, own_val, cond), F32),
        dma((6,)),
        dma((2, 2, 2)),
        dma((2, 2)),
        dma((2, 2)),
        dma((2,)),
        dma((8,)),
        dma((8,)),
    ]
    applied, intersection = pl.pallas_call(
        functools.partial(kernel, naux, ntr),
        out_shape=(
            jax.ShapeDtypeStruct((vectors, own_val, cond), F32),
            jax.ShapeDtypeStruct((vectors, vectors), F32),
        ),
        in_specs=[pl.BlockSpec(memory_space=pltpu.SMEM)] + [hbm] * 6,
        out_specs=(vmem, vmem),
        scratch_shapes=scratch,
        compiler_params=pltpu.CompilerParams(
            collective_id=0, has_side_effects=True, vmem_limit_bytes=48 * 1024 * 1024
        ),
    )(
        live_aux, *[pltpu.with_memory_space_constraint(x, pltpu.HBM) for x in (
            trial_vectors, energy_val.reshape(1, -1), energy_cond.reshape(1, -1), coef_occ, coef_virt, pair_coef)]
    )
    return pl.pallas_call(
        finish,
        out_shape=(
            jax.ShapeDtypeStruct(trial_vectors.shape, F32),
            jax.ShapeDtypeStruct((vectors, vectors), F32),
        ),
        in_specs=[vmem, vmem],
        out_specs=(vmem, vmem),
        compiler_params=pltpu.CompilerParams(vmem_limit_bytes=2 * 1024 * 1024),
    )(applied, intersection)


def solution(mesh):
    in_specs = (
        P("aux", None, "tr"),
        P("aux"),
        P("tr"),
        P("aux", None, None),
        P("aux", "tr", None),
        P("aux", "tr", None),
        P("aux"),
    )
    out_specs = (P("aux", None, "tr"), P())
    sizes = (mesh.shape["aux"], mesh.shape["tr"])
    return jax.shard_map(
        functools.partial(body, *sizes), mesh=mesh, in_specs=in_specs, out_specs=out_specs, check_vma=False
    )
```

```python
import contextlib
import functools

import jax
import jax.numpy as jnp
from jax import lax
from jax.experimental import pallas as pl
from jax.experimental.pallas import tpu as pltpu
from jax.sharding import PartitionSpec as P

F32 = jnp.float32
BF16 = jnp.bfloat16
BLEND = 64
LANES = 128
MESH = pl.DeviceIdType.MESH


def scope(name):
    return contextlib.nullcontext()


def kernel(
    naux, ntr,
    live_ref, trial_hbm, val_hbm, cond_hbm, occ_hbm, virt_hbm, pair_hbm,
    out_ref, inter_ref,
    trial_ref, val_ref, cond_ref, occ, virt, pair, blended, acc, mixed, trial_k, own_row,
    block_send, block_recv, cross_recv, mate_recv, proj_send, proj_recv, proj_all, proj_mate,
    sum_send, sum_recv, dots_send, dots_recv, core_recv, final_send, final_recv,
    load_sem, block_sem, proj_sem, sum_sem, dots_sem, extra_ssem, extra_rsem,
):
    g = lax.axis_index("grp")
    a = lax.axis_index("aux")
    t = lax.axis_index("tr")
    own_val, vectors, cond = trial_ref.shape
    half = vectors // 2
    size = half // 2
    slots, val, _ = occ.shape
    here = a * ntr + t

    arrays = ((trial_hbm, trial_ref), (val_hbm, val_ref), (cond_hbm, cond_ref),
              (pair_hbm, pair), (occ_hbm, occ), (virt_hbm, virt))
    loads = [pltpu.make_async_copy(src, dst, load_sem.at[n]) for n, (src, dst) in enumerate(arrays)]
    pair_copy, occ_copy, virt_copy = loads[3:]
    for copy in loads[:3]:
        copy.start()

    everyone = [(da, dt) for da in reversed(range(naux)) for dt in reversed(range(ntr)) if (da, dt) != (0, 0)]

    def along(d):
        assert naux & (naux - 1) == 0
        bits = [1 << i for i in range(naux.bit_length()) if d >> i & 1]
        return a + sum(bit * (1 - 2 * (a // bit % 2)) for bit in bits)

    def peer(da, dt):
        return {"aux": along(da), "tr": lax.rem(t + dt, ntr)}

    def send(src, dst, ssem, rsem, device):
        return pltpu.make_async_remote_copy(
            src_ref=src, dst_ref=dst, send_sem=ssem, recv_sem=rsem, device_id=device, device_id_type=MESH)

    def drain(refs, sem):
        return pltpu.make_async_copy(refs, refs, sem).wait

    mate = {"grp": 1 - g}
    barrier = pltpu.get_barrier_semaphore()
    with scope("signals"):
        greeted = [peer(da, 0) for da in reversed(range(1, naux))] + [peer(0, dt) for dt in range(1, ntr)] + [mate]
        for device in greeted:
            pl.semaphore_signal(barrier, inc=1, device_id=device, device_id_type=MESH)
    for copy in loads[3:]:
        copy.start()

    with scope("prep"):
        for copy in loads[:3]:
            copy.wait()
        square = (own_val, own_val)
        diagonal = lax.broadcasted_iota(jnp.int32, square, 0) == lax.broadcasted_iota(jnp.int32, square, 1)
        val_column = jnp.sum(jnp.where(diagonal, val_ref[...], 0.0), axis=1, keepdims=True)
        gap = cond_ref[...] - val_column
        for k in range(vectors):
            trial_k[k] = trial_ref[:, k, :]

    pairs = half * vectors
    lane = lax.broadcasted_iota(jnp.int32, (vectors, LANES), 1)
    vector = lax.broadcasted_iota(jnp.int32, (vectors, LANES), 0)

    def fold(x):
        return sum(x[:, n * LANES:(n + 1) * LANES] for n in range(x.shape[1] // LANES))

    def row_of(parts):
        rows = jnp.concatenate([jnp.sum(p, axis=0, keepdims=True) for part in parts for p in part], axis=0)
        n = lax.broadcasted_iota(jnp.int32, (pairs, LANES), 0)
        j = n // vectors
        place = j * vectors + lax.rem(n - j * vectors + g * half, vectors)
        spread = lax.broadcasted_iota(jnp.int32, (pairs, LANES), 1) == place
        return jnp.sum(jnp.where(spread, jnp.sum(rows, axis=1, keepdims=True), 0.0), axis=0, keepdims=True)

    def column(row, j):
        return jnp.sum(jnp.where(lane == j * vectors + vector, row, 0.0), axis=1, keepdims=True)

    def apply(it, x):
        finals = []

        def go(copy):
            copy.start()
            finals.append(copy.wait_send)
            return copy

        with scope("pack"):
            for h in range(2):
                block = jnp.concatenate(x[h * size:(h + 1) * size], axis=1).astype(BF16)
                block_send[it, h] = block
                block_recv[it, h, a] = block
        if it == 0:
            with scope("barrier"):
                pl.semaphore_wait(barrier, len(greeted))
        with scope("gather_issue"):
            for h in range(2):
                for d in reversed(range(1, naux)):
                    send(block_send.at[it, h], block_recv.at[it, h, a],
                         block_sem.at[0, it, h], block_sem.at[1, it, h], peer(d, 0)).start()
                blocks = block_recv.at[it, h, pl.ds(0, naux - 1)]
                finals.append(drain(blocks, block_sem.at[0, it, h]))

        with scope("project"):
            if it == 0:
                pair_copy.wait()
            for k in range(half):
                mixed[:, k, :] = x[k]
            proj = jnp.zeros((half, pair.shape[2]), F32)
            for v in range(own_val):
                proj += jnp.dot(mixed[v].astype(BF16), pair[v], preferred_element_type=F32)
            proj_send[it] = proj.astype(BF16)
            proj_recv[it, here] = proj.astype(BF16)

        if it == 0:
            with scope("mask"):
                occ_copy.wait()
                live = live_ref[0]
                step = min(16, slots)

                @pl.loop(0, slots // step)
                def _(i):
                    for q in range(step):
                        p = i * step + q
                        keep = jnp.full((val, val), jnp.where(p < live, 1.0, 0.0), F32).astype(BF16)
                        occ[p] = occ[p] * keep

                others = [trial_k[lax.rem(g * half + n, vectors)] for n in range(vectors)]
                own_row[...] = row_of([[fold(gap * others[j] * others[n]) for n in range(vectors)] for j in range(half)])

        crosses, mates = [], []
        mate_cross = send(cross_recv, mate_recv.at[1], extra_ssem.at[4], extra_rsem.at[4], mate)
        for h in range(2):
            with scope("gather_wait"):
                drain(block_recv.at[it, h, pl.ds(0, naux - 1)], block_sem.at[1, it, h])()
            if it == 0:
                crosses.append(go(send(
                    block_recv.at[0, h], cross_recv.at[h], extra_ssem.at[h], extra_rsem.at[h], peer(0, 1))))
                mates.append(go(send(
                    block_recv.at[0, h], mate_recv.at[0, h], extra_ssem.at[2 + h], extra_rsem.at[2 + h], mate)))
            if h == 1:
                with scope("proj_issue"):
                    for da, dt in everyone:
                        send(proj_send.at[it], proj_recv.at[it, here], proj_sem.at[0, it], proj_sem.at[1, it],
                             peer(da, dt)).start()
                    projections = proj_recv.at[it, pl.ds(0, len(everyone))]
                    finals.append(drain(projections, proj_sem.at[0, it]))
            with scope("blend"):
                wide = jnp.concatenate([block_recv[it, h, s].astype(F32) for s in range(naux)], axis=0).astype(BF16)
                columns = [wide[:, k * cond:(k + 1) * cond] for k in range(size)]

                @pl.when(t >= 0)
                def _():
                    i = 0
                    rows = occ[pl.ds(i * BLEND, BLEND)].reshape(BLEND * val, val)
                    for k in range(size):
                        b = jnp.dot(rows, columns[k], preferred_element_type=F32).astype(BF16)
                        for q in range(BLEND):
                            blended[i, (h * size + k) * val:(h * size + k + 1) * val,
                                    q * cond:(q + 1) * cond] = b[q * val:(q + 1) * val]

        if it == 0:
            with scope("virt_wait"):
                virt_copy.wait()

        part = val // 2
        owners = naux // 2

        def contract(rows, dt):
            start = pl.multiple_of(lax.rem(t + dt, ntr) * cond, cond)
            mixture = jnp.concatenate([
                jnp.concatenate([blended[i, ds, :] for i in range(slots // BLEND)], axis=1) for ds in rows], axis=0)
            acc[:mixture.shape[0]] = jnp.dot(
                mixture, virt[:, :, pl.ds(start, cond)].reshape(slots * cond, cond), preferred_element_type=F32)

        def pack(dt, s, rows):
            for k in range(half):
                sum_send[it, dt, s, :, k * cond:(k + 1) * cond] = acc[pl.ds(rows[k], own_val), :].astype(BF16)

        def post(dt, partners):
            for d in reversed(partners):
                send(sum_send.at[it, dt, along(d)], sum_recv.at[it, dt * naux + d],
                     sum_sem.at[0, it], sum_sem.at[1, it], peer(d, dt)).start()

        with scope("contract_a"):
            contract([pl.ds(0, half * val)], 1)
            for s in range(naux):
                pack(1, s, [k * val + s * own_val for k in range(half)])
            post(1, range(naux))
        with scope("contract_b"):
            @pl.loop(0, 2)
            def _(h):
                side = lax.rem(a // owners + 1 + h, 2)
                contract([
                    pl.ds(pl.multiple_of(k * val + side * part, part), part) for k in range(half)], 0)
                for s in range(owners):
                    pack(0, side * owners + s, [k * part + s * own_val for k in range(half)])

                @pl.when(h == 0)
                def _():
                    post(0, range(owners, naux))
                    if it == 0:
                        for copy in crosses:
                            copy.wait_recv()
                        mate_cross.start()

                @pl.when(h == 1)
                def _():
                    post(0, range(1, owners))

        with scope("sum_issue"):
            sums = sum_recv.at[it, pl.ds(1, len(everyone))]
            finals.append(drain(sums, sum_sem.at[0, it]))
            if it == 0:
                finals.append(mate_cross.wait_send)

        if it == 0:
            with scope("overlap"):
                for copy in mates:
                    copy.wait_recv()
                mate_cross.wait_recv()
                parts = [[jnp.zeros((own_val, LANES), F32)] * vectors for _ in range(half)]
                for dt in range(2):
                    for s in range(naux):
                        same = block_recv.at[0] if dt == 0 else cross_recv
                        both = [
                            ref[h, s, :, k * cond:(k + 1) * cond].astype(F32)
                            for ref in (same, mate_recv.at[dt]) for h in range(2) for k in range(size)]
                        for j in range(half):
                            mine = sum_send[0, dt, s, :, j * cond:(j + 1) * cond].astype(F32)
                            for n in range(vectors):
                                parts[j][n] = parts[j][n] + fold(mine * both[n])
                row = own_row[...] + row_of(parts)
                dots_send[...] = row
                dots_recv[here] = row
            with scope("dots_issue"):
                for da, dt in everyone:
                    send(dots_send, dots_recv.at[here], dots_sem.at[0], dots_sem.at[1], peer(da, dt)).start()

        with scope("exchange"):
            drain(projections, proj_sem.at[1, it])()
            proj = proj_recv[it, 0].astype(F32)
            for n in range(1, naux * ntr):
                proj += proj_recv[it, n].astype(F32)
            if it == 0:
                proj_all[...] = proj
                mate_proj = go(send(proj_all, proj_mate, extra_ssem.at[5], extra_rsem.at[5], mate))
            proj_b = proj.astype(BF16)
            for v in range(own_val):
                mixed[v] = lax.dot_general(
                    proj_b, pair[v], (((1,), (1,)), ((), ())), preferred_element_type=F32)
            local = [gap * x[k] + mixed[:, k, :] for k in range(half)]

        with scope("sum_wait"):
            drain(sums, sum_sem.at[1, it])()
        with scope("combine"):
            total = sum_send[it, 0, a].astype(F32)
            for n in range(1, naux * ntr):
                total += sum_recv[it, n].astype(F32)
            result = [local[k] + total[:, k * cond:(k + 1) * cond] for k in range(half)]
        return result, proj_b, mate_proj if it == 0 else None, finals

    first, proj_b, mate_proj, finals = apply(0, [trial_k[g * half + k] for k in range(half)])

    with scope("dots_wait"):
        mate_proj.wait_recv()
        dots = dots_recv.at[pl.ds(0, len(everyone))]
        drain(dots, dots_sem.at[1])()
        finals.append(drain(dots, dots_sem.at[0]))
    with scope("correct"):
        row = dots_recv[0]
        for n in range(1, naux * ntr):
            row += dots_recv[n]
        both = jnp.concatenate([proj_all[...], proj_mate[...]], axis=0)
        both = jnp.where(g == 0, both, jnp.concatenate([proj_mate[...], proj_all[...]], axis=0))
        inter = []
        for j in range(half):
            exchanged = jnp.sum(fold(both * proj_b[j:j + 1].astype(F32)), axis=1, keepdims=True)
            inter.append((column(row, j) + exchanged) / (naux * own_val * ntr * cond))
        square = jnp.zeros((vectors, LANES), F32)
        for j in range(half):
            square += jnp.where(lane == g * half + j, inter[j], 0.0)
        core_recv[0] = square
        core_dots = send(core_recv.at[0], core_recv.at[1], extra_ssem.at[6], extra_rsem.at[6], mate)
        core_dots.start()

        correction = []
        for j in range(half):
            fitted = trial_k[0] * inter[j][0:1, :]
            for k in range(1, vectors):
                fitted += trial_k[k] * inter[j][k:k + 1, :]
            correction.append((first[j] - fitted) / gap)

    second, _, _, more = apply(1, correction)
    with scope("final_pack"):
        for k in range(half):
            final_send[k] = second[k]
        final_copy = send(final_send, final_recv, extra_ssem.at[7], extra_rsem.at[7], mate)
        final_copy.start()
        for k in range(half):
            out_ref[g * half + k] = second[k]
    with scope("final_sends"):
        core_dots.wait()
        inter_ref[...] = (core_recv[0] + core_recv[1])[:, :vectors]
        for wait in finals + more:
            wait()
    with scope("final_wait"):
        final_copy.wait()
    with scope("final_store"):
        for k in range(half):
            out_ref[(1 - g) * half + k] = final_recv[k]


def finish(applied_ref, inter_ref, out_ref, inter_out_ref):
    for k in range(applied_ref.shape[0]):
        out_ref[:, k, :] = applied_ref[k]
    inter_out_ref[...] = inter_ref[...]


def body(naux, ntr, trial_vectors, energy_val, energy_cond, coef_occ, coef_virt, pair_coef, live_aux):
    own_val, vectors, cond = trial_vectors.shape
    slots, val, _ = coef_occ.shape
    naux_all = pair_coef.shape[2]
    half = vectors // 2
    peers = naux * ntr
    vmem = pl.BlockSpec(memory_space=pltpu.VMEM)
    hbm = pl.BlockSpec(memory_space=pltpu.HBM)
    dma = pltpu.SemaphoreType.DMA
    block = (own_val, half // 2 * cond)
    scratch = [
        pltpu.VMEM(trial_vectors.shape, F32),
        pltpu.VMEM((1, own_val), F32),
        pltpu.VMEM((1, cond), F32),
        pltpu.VMEM(coef_occ.shape, BF16),
        pltpu.VMEM(coef_virt.shape, BF16),
        pltpu.VMEM(pair_coef.shape, BF16),
        pltpu.VMEM((slots // BLEND, half * val, BLEND * cond), BF16),
        pltpu.VMEM((half * val, cond), F32),
        pltpu.VMEM((own_val, half, cond), F32),
        pltpu.VMEM((vectors, own_val, cond), F32),
        pltpu.VMEM((1, LANES), F32),
        pltpu.VMEM((2, 2, *block), BF16),
        pltpu.VMEM((2, 2, naux, *block), BF16),
        pltpu.VMEM((2, naux, *block), BF16),
        pltpu.VMEM((2, 2, naux, *block), BF16),
        pltpu.VMEM((2, half, naux_all), BF16),
        pltpu.VMEM((2, peers, half, naux_all), BF16),
        pltpu.VMEM((half, naux_all), F32),
        pltpu.VMEM((half, naux_all), F32),
        pltpu.VMEM((2, ntr, naux, own_val, half * cond), BF16),
        pltpu.VMEM((2, peers, own_val, half * cond), BF16),
        pltpu.VMEM((1, LANES), F32),
        pltpu.VMEM((peers, 1, LANES), F32),
        pltpu.VMEM((2, vectors, LANES), F32),
        pltpu.VMEM((half, own_val, cond), F32),
        pltpu.VMEM((half, own_val, cond), F32),
        dma((6,)),
        dma((2, 2, 2)),
        dma((2, 2)),
        dma((2, 2)),
        dma((2,)),
        dma((8,)),
        dma((8,)),
    ]
    applied, intersection = pl.pallas_call(
        functools.partial(kernel, naux, ntr),
        out_shape=(
            jax.ShapeDtypeStruct((vectors, own_val, cond), F32),
            jax.ShapeDtypeStruct((vectors, vectors), F32),
        ),
        in_specs=[pl.BlockSpec(memory_space=pltpu.SMEM)] + [hbm] * 6,
        out_specs=(vmem, vmem),
        scratch_shapes=scratch,
        compiler_params=pltpu.CompilerParams(
            collective_id=0, has_side_effects=True, vmem_limit_bytes=48 * 1024 * 1024
        ),
    )(
        live_aux, *[pltpu.with_memory_space_constraint(x, pltpu.HBM) for x in (
            trial_vectors, energy_val.reshape(1, -1), energy_cond.reshape(1, -1), coef_occ, coef_virt, pair_coef)]
    )
    return pl.pallas_call(
        finish,
        out_shape=(
            jax.ShapeDtypeStruct(trial_vectors.shape, F32),
            jax.ShapeDtypeStruct((vectors, vectors), F32),
        ),
        in_specs=[vmem, vmem],
        out_specs=(vmem, vmem),
        compiler_params=pltpu.CompilerParams(vmem_limit_bytes=2 * 1024 * 1024),
    )(applied, intersection)


def solution(mesh):
    in_specs = (
        P("aux", None, "tr"),
        P("aux"),
        P("tr"),
        P("aux", None, None),
        P("aux", "tr", None),
        P("aux", "tr", None),
        P("aux"),
    )
    out_specs = (P("aux", None, "tr"), P())
    sizes = (mesh.shape["aux"], mesh.shape["tr"])
    return jax.shard_map(
        functools.partial(body, *sizes), mesh=mesh, in_specs=in_specs, out_specs=out_specs, check_vma=False
    )
```

```python
import contextlib
import functools

import jax
import jax.numpy as jnp
from jax import lax
from jax.experimental import pallas as pl
from jax.experimental.pallas import tpu as pltpu
from jax.sharding import PartitionSpec as P

F32 = jnp.float32
BF16 = jnp.bfloat16
BLEND = 64
LANES = 128
MESH = pl.DeviceIdType.MESH


def scope(name):
    return contextlib.nullcontext()


def kernel(
    naux, ntr,
    live_ref, trial_hbm, val_hbm, cond_hbm, occ_hbm, virt_hbm, pair_hbm,
    out_ref, inter_ref,
    trial_ref, val_ref, cond_ref, occ, virt, pair, blended, acc, mixed, trial_k, own_row,
    block_send, block_recv, cross_recv, mate_recv, proj_send, proj_recv, proj_all, proj_mate,
    sum_send, sum_recv, dots_send, dots_recv, core_recv, final_send, final_recv,
    load_sem, block_sem, proj_sem, sum_sem, dots_sem, extra_ssem, extra_rsem,
):
    g = lax.axis_index("grp")
    a = lax.axis_index("aux")
    t = lax.axis_index("tr")
    own_val, vectors, cond = trial_ref.shape
    half = vectors // 2
    size = half // 2
    slots, val, _ = occ.shape
    here = a * ntr + t

    arrays = ((trial_hbm, trial_ref), (val_hbm, val_ref), (cond_hbm, cond_ref),
              (pair_hbm, pair), (occ_hbm, occ)) + tuple(
        (virt_hbm.at[:, :, pl.ds(pl.multiple_of(lax.rem(t + dt, ntr) * cond, cond), cond)], virt.at[dt])
        for dt in (1, 0))
    loads = [pltpu.make_async_copy(src, dst, load_sem.at[n]) for n, (src, dst) in enumerate(arrays)]
    pair_copy, occ_copy, *virt_copies = loads[3:]
    for copy in loads[:3]:
        copy.start()

    everyone = [(da, dt) for da in reversed(range(naux)) for dt in reversed(range(ntr)) if (da, dt) != (0, 0)]

    def along(d):
        assert naux & (naux - 1) == 0
        bits = [1 << i for i in range(naux.bit_length()) if d >> i & 1]
        return a + sum(bit * (1 - 2 * (a // bit % 2)) for bit in bits)

    def peer(da, dt):
        return {"aux": along(da), "tr": lax.rem(t + dt, ntr)}

    def send(src, dst, ssem, rsem, device):
        return pltpu.make_async_remote_copy(
            src_ref=src, dst_ref=dst, send_sem=ssem, recv_sem=rsem, device_id=device, device_id_type=MESH)

    def drain(refs, sem):
        return pltpu.make_async_copy(refs, refs, sem).wait

    mate = {"grp": 1 - g}
    barrier = pltpu.get_barrier_semaphore()
    with scope("signals"):
        greeted = [peer(da, 0) for da in reversed(range(1, naux))] + [peer(0, dt) for dt in range(1, ntr)] + [mate]
        for device in greeted:
            pl.semaphore_signal(barrier, inc=1, device_id=device, device_id_type=MESH)
    for copy in loads[3:]:
        copy.start()

    with scope("prep"):
        for copy in loads[:3]:
            copy.wait()
        square = (own_val, own_val)
        diagonal = lax.broadcasted_iota(jnp.int32, square, 0) == lax.broadcasted_iota(jnp.int32, square, 1)
        val_column = jnp.sum(jnp.where(diagonal, val_ref[...], 0.0), axis=1, keepdims=True)
        gap = cond_ref[...] - val_column
        for k in range(vectors):
            trial_k[k] = trial_ref[:, k, :]

    pairs = half * vectors
    lane = lax.broadcasted_iota(jnp.int32, (vectors, LANES), 1)
    vector = lax.broadcasted_iota(jnp.int32, (vectors, LANES), 0)

    def fold(x):
        return sum(x[:, n * LANES:(n + 1) * LANES] for n in range(x.shape[1] // LANES))

    def row_of(parts):
        rows = jnp.concatenate([jnp.sum(p, axis=0, keepdims=True) for part in parts for p in part], axis=0)
        n = lax.broadcasted_iota(jnp.int32, (pairs, LANES), 0)
        j = n // vectors
        place = j * vectors + lax.rem(n - j * vectors + g * half, vectors)
        spread = lax.broadcasted_iota(jnp.int32, (pairs, LANES), 1) == place
        return jnp.sum(jnp.where(spread, jnp.sum(rows, axis=1, keepdims=True), 0.0), axis=0, keepdims=True)

    def column(row, j):
        return jnp.sum(jnp.where(lane == j * vectors + vector, row, 0.0), axis=1, keepdims=True)

    def apply(it, x):
        finals = []

        def go(copy):
            copy.start()
            finals.append(copy.wait_send)
            return copy

        with scope("pack"):
            for h in range(2):
                block = jnp.concatenate(x[h * size:(h + 1) * size], axis=1).astype(BF16)
                block_send[it, h] = block
                block_recv[it, h, a] = block
        if it == 0:
            with scope("barrier"):
                pl.semaphore_wait(barrier, len(greeted))
        with scope("gather_issue"):
            for h in range(2):
                for d in reversed(range(1, naux)):
                    send(block_send.at[it, h], block_recv.at[it, h, a],
                         block_sem.at[0, it, h], block_sem.at[1, it, h], peer(d, 0)).start()
                blocks = block_recv.at[it, h, pl.ds(0, naux - 1)]
                finals.append(drain(blocks, block_sem.at[0, it, h]))

        with scope("project"):
            if it == 0:
                pair_copy.wait()
            for k in range(half):
                mixed[:, k, :] = x[k]
            proj = jnp.zeros((half, pair.shape[2]), F32)
            for v in range(own_val):
                proj += jnp.dot(mixed[v].astype(BF16), pair[v], preferred_element_type=F32)
            proj_send[it] = proj.astype(BF16)
            proj_recv[it, here] = proj.astype(BF16)

        if it == 0:
            with scope("mask"):
                occ_copy.wait()
                live = live_ref[0]
                step = min(16, slots)

                @pl.loop(0, slots // step)
                def _(i):
                    for q in range(step):
                        p = i * step + q
                        keep = jnp.full((val, val), jnp.where(p < live, 1.0, 0.0), F32).astype(BF16)
                        occ[p] = occ[p] * keep

                others = [trial_k[lax.rem(g * half + n, vectors)] for n in range(vectors)]
                own_row[...] = row_of([[fold(gap * others[j] * others[n]) for n in range(vectors)] for j in range(half)])

        crosses, mates = [], []
        mate_cross = send(cross_recv, mate_recv.at[1], extra_ssem.at[4], extra_rsem.at[4], mate)
        for h in range(2):
            with scope("gather_wait"):
                drain(block_recv.at[it, h, pl.ds(0, naux - 1)], block_sem.at[1, it, h])()
            if it == 0:
                crosses.append(go(send(
                    block_recv.at[0, h], cross_recv.at[h], extra_ssem.at[h], extra_rsem.at[h], peer(0, 1))))
                mates.append(go(send(
                    block_recv.at[0, h], mate_recv.at[0, h], extra_ssem.at[2 + h], extra_rsem.at[2 + h], mate)))
            if h == 1:
                with scope("proj_issue"):
                    for da, dt in everyone:
                        send(proj_send.at[it], proj_recv.at[it, here], proj_sem.at[0, it], proj_sem.at[1, it],
                             peer(da, dt)).start()
                    projections = proj_recv.at[it, pl.ds(0, len(everyone))]
                    finals.append(drain(projections, proj_sem.at[0, it]))
            with scope("blend"):
                wide = jnp.concatenate([block_recv[it, h, s].astype(F32) for s in range(naux)], axis=0).astype(BF16)
                columns = [wide[:, k * cond:(k + 1) * cond] for k in range(size)]

                @pl.when((t, a)[h] >= 0)
                def _():
                    i = 0
                    rows = occ[pl.ds(i * BLEND, BLEND)].reshape(BLEND * val, val)
                    for k in range(size):
                        b = jnp.dot(rows, columns[k], preferred_element_type=F32).astype(BF16)
                        for q in range(BLEND):
                            blended[i, (h * size + k) * val:(h * size + k + 1) * val,
                                    q * cond:(q + 1) * cond] = b[q * val:(q + 1) * val]

        if it == 0:
            with scope("virt_wait"):
                for copy in virt_copies:
                    copy.wait()

        part = val // 2
        owners = naux // 2

        def contract(rows, dt):
            mixture = jnp.concatenate([
                jnp.concatenate([blended[i, ds, :] for i in range(slots // BLEND)], axis=1) for ds in rows], axis=0)
            acc[:mixture.shape[0]] = jnp.dot(
                mixture, virt[dt].reshape(slots * cond, cond), preferred_element_type=F32)

        def pack(dt, s, rows):
            for k in range(half):
                sum_send[it, dt, s, :, k * cond:(k + 1) * cond] = acc[pl.ds(rows[k], own_val), :].astype(BF16)

        def post(dt, partners):
            for d in reversed(partners):
                send(sum_send.at[it, dt, along(d)], sum_recv.at[it, dt * naux + d],
                     sum_sem.at[0, it], sum_sem.at[1, it], peer(d, dt)).start()

        with scope("contract_a"):
            @pl.when(g >= 0)
            def _():
                contract([pl.ds(0, half * val)], 1)
                for s in range(naux):
                    pack(1, s, [k * val + s * own_val for k in range(half)])
                post(1, range(naux))
        with scope("contract_b"):
            @pl.loop(0, 2)
            def _(h):
                side = lax.rem(a // owners + 1 + h, 2)
                contract([
                    pl.ds(pl.multiple_of(k * val + side * part, part), part) for k in range(half)], 0)
                for s in range(owners):
                    pack(0, side * owners + s, [k * part + s * own_val for k in range(half)])

                @pl.when(h == 0)
                def _():
                    post(0, range(owners, naux))
                    if it == 0:
                        for copy in crosses:
                            copy.wait_recv()
                        mate_cross.start()

                @pl.when(h == 1)
                def _():
                    post(0, range(1, owners))

        with scope("sum_issue"):
            sums = sum_recv.at[it, pl.ds(1, len(everyone))]
            finals.append(drain(sums, sum_sem.at[0, it]))
            if it == 0:
                finals.append(mate_cross.wait_send)

        if it == 0:
            with scope("overlap"):
                for copy in mates:
                    copy.wait_recv()
                mate_cross.wait_recv()
                parts = [[jnp.zeros((own_val, LANES), F32)] * vectors for _ in range(half)]
                for dt in range(2):
                    for s in range(naux):
                        same = block_recv.at[0] if dt == 0 else cross_recv
                        both = [
                            ref[h, s, :, k * cond:(k + 1) * cond].astype(F32)
                            for ref in (same, mate_recv.at[dt]) for h in range(2) for k in range(size)]
                        for j in range(half):
                            mine = sum_send[0, dt, s, :, j * cond:(j + 1) * cond].astype(F32)
                            for n in range(vectors):
                                parts[j][n] = parts[j][n] + fold(mine * both[n])
                row = own_row[...] + row_of(parts)
                dots_send[...] = row
                dots_recv[here] = row
            with scope("dots_issue"):
                for da, dt in everyone:
                    send(dots_send, dots_recv.at[here], dots_sem.at[0], dots_sem.at[1], peer(da, dt)).start()

        with scope("exchange"):
            drain(projections, proj_sem.at[1, it])()
            proj = proj_recv[it, 0].astype(F32)
            for n in range(1, naux * ntr):
                proj += proj_recv[it, n].astype(F32)
            if it == 0:
                proj_all[...] = proj
                mate_proj = go(send(proj_all, proj_mate, extra_ssem.at[5], extra_rsem.at[5], mate))
            proj_b = proj.astype(BF16)
            for v in range(own_val):
                mixed[v] = lax.dot_general(
                    proj_b, pair[v], (((1,), (1,)), ((), ())), preferred_element_type=F32)
            local = [gap * x[k] + mixed[:, k, :] for k in range(half)]

        with scope("sum_wait"):
            drain(sums, sum_sem.at[1, it])()
        with scope("combine"):
            total = sum_send[it, 0, a].astype(F32)
            for n in range(1, naux * ntr):
                total += sum_recv[it, n].astype(F32)
            result = [local[k] + total[:, k * cond:(k + 1) * cond] for k in range(half)]
        return result, proj_b, mate_proj if it == 0 else None, finals

    first, proj_b, mate_proj, finals = apply(0, [trial_k[g * half + k] for k in range(half)])

    with scope("dots_wait"):
        mate_proj.wait_recv()
        dots = dots_recv.at[pl.ds(0, len(everyone))]
        drain(dots, dots_sem.at[1])()
        finals.append(drain(dots, dots_sem.at[0]))
    with scope("correct"):
        row = dots_recv[0]
        for n in range(1, naux * ntr):
            row += dots_recv[n]
        both = jnp.concatenate([proj_all[...], proj_mate[...]], axis=0)
        both = jnp.where(g == 0, both, jnp.concatenate([proj_mate[...], proj_all[...]], axis=0))
        inter = []
        for j in range(half):
            exchanged = jnp.sum(fold(both * proj_b[j:j + 1].astype(F32)), axis=1, keepdims=True)
            inter.append((column(row, j) + exchanged) / (naux * own_val * ntr * cond))
        square = jnp.zeros((vectors, LANES), F32)
        for j in range(half):
            square += jnp.where(lane == g * half + j, inter[j], 0.0)
        core_recv[0] = square
        core_dots = send(core_recv.at[0], core_recv.at[1], extra_ssem.at[6], extra_rsem.at[6], mate)
        core_dots.start()

        correction = []
        for j in range(half):
            fitted = trial_k[0] * inter[j][0:1, :]
            for k in range(1, vectors):
                fitted += trial_k[k] * inter[j][k:k + 1, :]
            correction.append((first[j] - fitted) / gap)

    second, _, _, more = apply(1, correction)
    with scope("final_pack"):
        for k in range(half):
            final_send[k] = second[k]
        final_copy = send(final_send, final_recv, extra_ssem.at[7], extra_rsem.at[7], mate)
        final_copy.start()
        for k in range(half):
            out_ref[g * half + k] = second[k]
    with scope("final_sends"):
        core_dots.wait()
        inter_ref[...] = (core_recv[0] + core_recv[1])[:, :vectors]
        for wait in finals + more:
            wait()
    with scope("final_wait"):
        final_copy.wait()
    with scope("final_store"):
        for k in range(half):
            out_ref[(1 - g) * half + k] = final_recv[k]


def finish(applied_ref, inter_ref, out_ref, inter_out_ref):
    for k in range(applied_ref.shape[0]):
        out_ref[:, k, :] = applied_ref[k]
    inter_out_ref[...] = inter_ref[...]


def body(naux, ntr, trial_vectors, energy_val, energy_cond, coef_occ, coef_virt, pair_coef, live_aux):
    own_val, vectors, cond = trial_vectors.shape
    slots, val, _ = coef_occ.shape
    naux_all = pair_coef.shape[2]
    half = vectors // 2
    peers = naux * ntr
    vmem = pl.BlockSpec(memory_space=pltpu.VMEM)
    hbm = pl.BlockSpec(memory_space=pltpu.HBM)
    dma = pltpu.SemaphoreType.DMA
    block = (own_val, half // 2 * cond)
    scratch = [
        pltpu.VMEM(trial_vectors.shape, F32),
        pltpu.VMEM((1, own_val), F32),
        pltpu.VMEM((1, cond), F32),
        pltpu.VMEM(coef_occ.shape, BF16),
        pltpu.VMEM((ntr, slots, cond, cond), BF16),
        pltpu.VMEM(pair_coef.shape, BF16),
        pltpu.VMEM((slots // BLEND, half * val, BLEND * cond), BF16),
        pltpu.VMEM((half * val, cond), F32),
        pltpu.VMEM((own_val, half, cond), F32),
        pltpu.VMEM((vectors, own_val, cond), F32),
        pltpu.VMEM((1, LANES), F32),
        pltpu.VMEM((2, 2, *block), BF16),
        pltpu.VMEM((2, 2, naux, *block), BF16),
        pltpu.VMEM((2, naux, *block), BF16),
        pltpu.VMEM((2, 2, naux, *block), BF16),
        pltpu.VMEM((2, half, naux_all), BF16),
        pltpu.VMEM((2, peers, half, naux_all), BF16),
        pltpu.VMEM((half, naux_all), F32),
        pltpu.VMEM((half, naux_all), F32),
        pltpu.VMEM((2, ntr, naux, own_val, half * cond), BF16),
        pltpu.VMEM((2, peers, own_val, half * cond), BF16),
        pltpu.VMEM((1, LANES), F32),
        pltpu.VMEM((peers, 1, LANES), F32),
        pltpu.VMEM((2, vectors, LANES), F32),
        pltpu.VMEM((half, own_val, cond), F32),
        pltpu.VMEM((half, own_val, cond), F32),
        dma((7,)),
        dma((2, 2, 2)),
        dma((2, 2)),
        dma((2, 2)),
        dma((2,)),
        dma((8,)),
        dma((8,)),
    ]
    applied, intersection = pl.pallas_call(
        functools.partial(kernel, naux, ntr),
        out_shape=(
            jax.ShapeDtypeStruct((vectors, own_val, cond), F32),
            jax.ShapeDtypeStruct((vectors, vectors), F32),
        ),
        in_specs=[pl.BlockSpec(memory_space=pltpu.SMEM)] + [hbm] * 6,
        out_specs=(vmem, vmem),
        scratch_shapes=scratch,
        compiler_params=pltpu.CompilerParams(
            collective_id=0, has_side_effects=True, vmem_limit_bytes=48 * 1024 * 1024
        ),
    )(
        live_aux, *[pltpu.with_memory_space_constraint(x, pltpu.HBM) for x in (
            trial_vectors, energy_val.reshape(1, -1), energy_cond.reshape(1, -1), coef_occ, coef_virt, pair_coef)]
    )
    return pl.pallas_call(
        finish,
        out_shape=(
            jax.ShapeDtypeStruct(trial_vectors.shape, F32),
            jax.ShapeDtypeStruct((vectors, vectors), F32),
        ),
        in_specs=[vmem, vmem],
        out_specs=(vmem, vmem),
        compiler_params=pltpu.CompilerParams(vmem_limit_bytes=2 * 1024 * 1024),
    )(applied, intersection)


def solution(mesh):
    in_specs = (
        P("aux", None, "tr"),
        P("aux"),
        P("tr"),
        P("aux", None, None),
        P("aux", "tr", None),
        P("aux", "tr", None),
        P("aux"),
    )
    out_specs = (P("aux", None, "tr"), P())
    sizes = (mesh.shape["aux"], mesh.shape["tr"])
    return jax.shard_map(
        functools.partial(body, *sizes), mesh=mesh, in_specs=in_specs, out_specs=out_specs, check_vma=False
    )
```

```python
import contextlib
import functools

import jax
import jax.numpy as jnp
from jax import lax
from jax.experimental import pallas as pl
from jax.experimental.pallas import tpu as pltpu
from jax.sharding import PartitionSpec as P

F32 = jnp.float32
BF16 = jnp.bfloat16
BLEND = 64
LANES = 128
MESH = pl.DeviceIdType.MESH


def scope(name):
    return contextlib.nullcontext()


def kernel(
    naux, ntr,
    live_ref, trial_hbm, val_hbm, cond_hbm, occ_hbm, virt_hbm, pair_hbm,
    out_ref, inter_ref,
    trial_ref, val_ref, cond_ref, occ, virt, pair, blended, acc, mixed, trial_k, own_row,
    block_send, block_recv, cross_recv, mate_recv, proj_send, proj_recv, proj_all, proj_mate,
    sum_send, sum_recv, dots_send, dots_recv, core_recv, final_send, final_recv,
    load_sem, block_sem, proj_sem, sum_sem, dots_sem, extra_ssem, extra_rsem,
):
    g = lax.axis_index("grp")
    a = lax.axis_index("aux")
    t = lax.axis_index("tr")
    own_val, vectors, cond = trial_ref.shape
    half = vectors // 2
    size = half // 2
    slots, val, _ = occ.shape
    here = a * ntr + t

    arrays = ((trial_hbm, trial_ref), (val_hbm, val_ref), (cond_hbm, cond_ref),
              (pair_hbm, pair), (occ_hbm, occ)) + tuple(
        (virt_hbm.at[:, :, pl.ds(pl.multiple_of(lax.rem(t + dt, ntr) * cond, cond), cond)], virt.at[dt])
        for dt in (1, 0))
    loads = [pltpu.make_async_copy(src, dst, load_sem.at[n]) for n, (src, dst) in enumerate(arrays)]
    pair_copy, occ_copy, *virt_copies = loads[3:]
    for copy in loads[:3]:
        copy.start()

    everyone = [(da, dt) for da in reversed(range(naux)) for dt in reversed(range(ntr)) if (da, dt) != (0, 0)]

    def along(d):
        assert naux & (naux - 1) == 0
        bits = [1 << i for i in range(naux.bit_length()) if d >> i & 1]
        return a + sum(bit * (1 - 2 * (a // bit % 2)) for bit in bits)

    def peer(da, dt):
        return {"aux": along(da), "tr": lax.rem(t + dt, ntr)}

    def send(src, dst, ssem, rsem, device):
        return pltpu.make_async_remote_copy(
            src_ref=src, dst_ref=dst, send_sem=ssem, recv_sem=rsem, device_id=device, device_id_type=MESH)

    def drain(refs, sem):
        return pltpu.make_async_copy(refs, refs, sem).wait

    mate = {"grp": 1 - g}
    barrier = pltpu.get_barrier_semaphore()
    with scope("signals"):
        greeted = [peer(da, 0) for da in reversed(range(1, naux))] + [peer(0, dt) for dt in range(1, ntr)] + [mate]
        for device in greeted:
            pl.semaphore_signal(barrier, inc=1, device_id=device, device_id_type=MESH)
    for copy in loads[3:]:
        copy.start()

    with scope("prep"):
        for copy in loads[:3]:
            copy.wait()
        square = (own_val, own_val)
        diagonal = lax.broadcasted_iota(jnp.int32, square, 0) == lax.broadcasted_iota(jnp.int32, square, 1)
        val_column = jnp.sum(jnp.where(diagonal, val_ref[...], 0.0), axis=1, keepdims=True)
        gap = cond_ref[...] - val_column
        for k in range(vectors):
            trial_k[k] = trial_ref[:, k, :]

    pairs = half * vectors
    lane = lax.broadcasted_iota(jnp.int32, (vectors, LANES), 1)
    vector = lax.broadcasted_iota(jnp.int32, (vectors, LANES), 0)

    def fold(x):
        return sum(x[:, n * LANES:(n + 1) * LANES] for n in range(x.shape[1] // LANES))

    def row_of(parts):
        rows = jnp.concatenate([jnp.sum(p, axis=0, keepdims=True) for part in parts for p in part], axis=0)
        n = lax.broadcasted_iota(jnp.int32, (pairs, LANES), 0)
        j = n // vectors
        place = j * vectors + lax.rem(n - j * vectors + g * half, vectors)
        spread = lax.broadcasted_iota(jnp.int32, (pairs, LANES), 1) == place
        return jnp.sum(jnp.where(spread, jnp.sum(rows, axis=1, keepdims=True), 0.0), axis=0, keepdims=True)

    def column(row, j):
        return jnp.sum(jnp.where(lane == j * vectors + vector, row, 0.0), axis=1, keepdims=True)

    def apply(it, x):
        finals = []

        def go(copy):
            copy.start()
            finals.append(copy.wait_send)
            return copy

        with scope("pack"):
            for h in range(2):
                block = jnp.concatenate(x[h * size:(h + 1) * size], axis=1).astype(BF16)
                block_send[it, h] = block
                block_recv[it, h, a] = block
        if it == 0:
            with scope("barrier"):
                pl.semaphore_wait(barrier, len(greeted))
        with scope("gather_issue"):
            for h in range(2):
                for d in reversed(range(1, naux)):
                    send(block_send.at[it, h], block_recv.at[it, h, a],
                         block_sem.at[0, it, h], block_sem.at[1, it, h], peer(d, 0)).start()
                blocks = block_recv.at[it, h, pl.ds(0, naux - 1)]
                finals.append(drain(blocks, block_sem.at[0, it, h]))

        with scope("project"):
            if it == 0:
                pair_copy.wait()
            for k in range(half):
                mixed[:, k, :] = x[k]
            proj = jnp.zeros((half, pair.shape[2]), F32)
            for v in range(own_val):
                proj += jnp.dot(mixed[v].astype(BF16), pair[v], preferred_element_type=F32)
            proj_send[it] = proj.astype(BF16)
            proj_recv[it, here] = proj.astype(BF16)

        if it == 0:
            with scope("mask"):
                occ_copy.wait()
                live = live_ref[0]
                step = min(16, slots)

                @pl.loop(0, slots // step)
                def _(i):
                    for q in range(step):
                        p = i * step + q
                        keep = jnp.full((val, val), jnp.where(p < live, 1.0, 0.0), F32).astype(BF16)
                        occ[p] = occ[p] * keep

                others = [trial_k[lax.rem(g * half + n, vectors)] for n in range(vectors)]
                own_row[...] = row_of([[fold(gap * others[j] * others[n]) for n in range(vectors)] for j in range(half)])

        crosses, mates = [], []
        mate_cross = send(cross_recv, mate_recv.at[1], extra_ssem.at[4], extra_rsem.at[4], mate)
        for h in range(2):
            with scope("gather_wait"):
                drain(block_recv.at[it, h, pl.ds(0, naux - 1)], block_sem.at[1, it, h])()
            if it == 0:
                crosses.append(go(send(
                    block_recv.at[0, h], cross_recv.at[h], extra_ssem.at[h], extra_rsem.at[h], peer(0, 1))))
                mates.append(go(send(
                    block_recv.at[0, h], mate_recv.at[0, h], extra_ssem.at[2 + h], extra_rsem.at[2 + h], mate)))
            if h == 1:
                with scope("proj_issue"):
                    for da, dt in everyone:
                        send(proj_send.at[it], proj_recv.at[it, here], proj_sem.at[0, it], proj_sem.at[1, it],
                             peer(da, dt)).start()
                    projections = proj_recv.at[it, pl.ds(0, len(everyone))]
                    finals.append(drain(projections, proj_sem.at[0, it]))
            with scope("blend"):
                wide = jnp.concatenate([block_recv[it, h, s].astype(F32) for s in range(naux)], axis=0).astype(BF16)
                columns = [wide[:, k * cond:(k + 1) * cond] for k in range(size)]

                @pl.when((t, a)[h] >= 0)
                def _():
                    i = 0
                    rows = occ[pl.ds(i * BLEND, BLEND)].reshape(BLEND * val, val)
                    for k in range(size):
                        b = jnp.dot(rows, columns[k], preferred_element_type=F32).astype(BF16)
                        for q in range(BLEND):
                            blended[i, (h * size + k) * val:(h * size + k + 1) * val,
                                    q * cond:(q + 1) * cond] = b[q * val:(q + 1) * val]

        if it == 0:
            with scope("virt_wait"):
                for copy in virt_copies:
                    copy.wait()

        part = val // 2
        owners = naux // 2

        def contract(rows, dt):
            mixture = jnp.concatenate([
                jnp.concatenate([blended[i, ds, :] for i in range(slots // BLEND)], axis=1) for ds in rows], axis=0)
            acc[:mixture.shape[0]] = jnp.dot(
                mixture, virt[dt].reshape(slots * cond, cond), preferred_element_type=F32)

        def pack(dt, s, rows):
            for k in range(half):
                sum_send[it, dt, s, :, k * cond:(k + 1) * cond] = acc[pl.ds(rows[k], own_val), :].astype(BF16)

        def post(dt, partners):
            for d in reversed(partners):
                send(sum_send.at[it, dt, along(d)], sum_recv.at[it, dt * naux + d],
                     sum_sem.at[0, it], sum_sem.at[1, it], peer(d, dt)).start()

        with scope("contract_a"):
            @pl.when(g >= 0)
            def _():
                contract([pl.ds(0, half * val)], 1)
                for s in range(naux):
                    pack(1, s, [k * val + s * own_val for k in range(half)])
                post(1, range(naux))
        if it == 0:
            with scope("cross_wait"):
                for copy in crosses:
                    copy.wait_recv()
                mate_cross.start()
            with scope("contract_b"):
                @pl.when(t >= 0)
                def _():
                    contract([pl.ds(0, half * val)], 0)
                    for s in range(naux):
                        pack(0, s, [k * val + s * own_val for k in range(half)])
        else:
            with scope("contract_b"):
                @pl.loop(0, 2)
                def _(h):
                    side = lax.rem(a // owners + 1 + h, 2)
                    contract([
                        pl.ds(pl.multiple_of(k * val + side * part, part), part) for k in range(half)], 0)
                    for s in range(owners):
                        pack(0, side * owners + s, [k * part + s * own_val for k in range(half)])

                    @pl.when(h == 0)
                    def _():
                        post(0, range(owners, naux))

                    @pl.when(h == 1)
                    def _():
                        post(0, range(1, owners))

        with scope("sum_issue"):
            sums = sum_recv.at[it, pl.ds(1, len(everyone))]
            finals.append(drain(sums, sum_sem.at[0, it]))
            if it == 0:
                finals.append(mate_cross.wait_send)

        if it == 0:
            with scope("overlap"):
                for copy in mates:
                    copy.wait_recv()
                mate_cross.wait_recv()
                parts = [[jnp.zeros((own_val, LANES), F32)] * vectors for _ in range(half)]
                for dt in range(2):
                    for s in range(naux):
                        same = block_recv.at[0] if dt == 0 else cross_recv
                        both = [
                            ref[h, s, :, k * cond:(k + 1) * cond].astype(F32)
                            for ref in (same, mate_recv.at[dt]) for h in range(2) for k in range(size)]
                        for j in range(half):
                            mine = sum_send[0, dt, s, :, j * cond:(j + 1) * cond].astype(F32)
                            for n in range(vectors):
                                parts[j][n] = parts[j][n] + fold(mine * both[n])
                row = own_row[...] + row_of(parts)
                dots_send[...] = row
                dots_recv[here] = row
            with scope("dots_issue"):
                for da, dt in everyone:
                    send(dots_send, dots_recv.at[here], dots_sem.at[0], dots_sem.at[1], peer(da, dt)).start()
                post(0, range(1, naux))

        with scope("exchange"):
            drain(projections, proj_sem.at[1, it])()
            proj = proj_recv[it, 0].astype(F32)
            for n in range(1, naux * ntr):
                proj += proj_recv[it, n].astype(F32)
            if it == 0:
                proj_all[...] = proj
                mate_proj = go(send(proj_all, proj_mate, extra_ssem.at[5], extra_rsem.at[5], mate))
            proj_b = proj.astype(BF16)
            for v in range(own_val):
                mixed[v] = lax.dot_general(
                    proj_b, pair[v], (((1,), (1,)), ((), ())), preferred_element_type=F32)
            local = [gap * x[k] + mixed[:, k, :] for k in range(half)]

        with scope("sum_wait"):
            drain(sums, sum_sem.at[1, it])()
        with scope("combine"):
            total = sum_send[it, 0, a].astype(F32)
            for n in range(1, naux * ntr):
                total += sum_recv[it, n].astype(F32)
            result = [local[k] + total[:, k * cond:(k + 1) * cond] for k in range(half)]
        return result, proj_b, mate_proj if it == 0 else None, finals

    first, proj_b, mate_proj, finals = apply(0, [trial_k[g * half + k] for k in range(half)])

    with scope("dots_wait"):
        mate_proj.wait_recv()
        dots = dots_recv.at[pl.ds(0, len(everyone))]
        drain(dots, dots_sem.at[1])()
        finals.append(drain(dots, dots_sem.at[0]))
    with scope("correct"):
        row = dots_recv[0]
        for n in range(1, naux * ntr):
            row += dots_recv[n]
        both = jnp.concatenate([proj_all[...], proj_mate[...]], axis=0)
        both = jnp.where(g == 0, both, jnp.concatenate([proj_mate[...], proj_all[...]], axis=0))
        inter = []
        for j in range(half):
            exchanged = jnp.sum(fold(both * proj_b[j:j + 1].astype(F32)), axis=1, keepdims=True)
            inter.append((column(row, j) + exchanged) / (naux * own_val * ntr * cond))
        square = jnp.zeros((vectors, LANES), F32)
        for j in range(half):
            square += jnp.where(lane == g * half + j, inter[j], 0.0)
        core_recv[0] = square
        core_dots = send(core_recv.at[0], core_recv.at[1], extra_ssem.at[6], extra_rsem.at[6], mate)
        core_dots.start()

        correction = []
        for j in range(half):
            fitted = trial_k[0] * inter[j][0:1, :]
            for k in range(1, vectors):
                fitted += trial_k[k] * inter[j][k:k + 1, :]
            correction.append((first[j] - fitted) / gap)

    second, _, _, more = apply(1, correction)
    with scope("final_pack"):
        for k in range(half):
            final_send[k] = second[k]
        final_copy = send(final_send, final_recv, extra_ssem.at[7], extra_rsem.at[7], mate)
        final_copy.start()
        for k in range(half):
            out_ref[g * half + k] = second[k]
    with scope("final_sends"):
        core_dots.wait()
        inter_ref[...] = (core_recv[0] + core_recv[1])[:, :vectors]
        for wait in finals + more:
            wait()
    with scope("final_wait"):
        final_copy.wait()
    with scope("final_store"):
        for k in range(half):
            out_ref[(1 - g) * half + k] = final_recv[k]


def finish(applied_ref, inter_ref, out_ref, inter_out_ref):
    for k in range(applied_ref.shape[0]):
        out_ref[:, k, :] = applied_ref[k]
    inter_out_ref[...] = inter_ref[...]


def body(naux, ntr, trial_vectors, energy_val, energy_cond, coef_occ, coef_virt, pair_coef, live_aux):
    own_val, vectors, cond = trial_vectors.shape
    slots, val, _ = coef_occ.shape
    naux_all = pair_coef.shape[2]
    half = vectors // 2
    peers = naux * ntr
    vmem = pl.BlockSpec(memory_space=pltpu.VMEM)
    hbm = pl.BlockSpec(memory_space=pltpu.HBM)
    dma = pltpu.SemaphoreType.DMA
    block = (own_val, half // 2 * cond)
    scratch = [
        pltpu.VMEM(trial_vectors.shape, F32),
        pltpu.VMEM((1, own_val), F32),
        pltpu.VMEM((1, cond), F32),
        pltpu.VMEM(coef_occ.shape, BF16),
        pltpu.VMEM((ntr, slots, cond, cond), BF16),
        pltpu.VMEM(pair_coef.shape, BF16),
        pltpu.VMEM((slots // BLEND, half * val, BLEND * cond), BF16),
        pltpu.VMEM((half * val, cond), F32),
        pltpu.VMEM((own_val, half, cond), F32),
        pltpu.VMEM((vectors, own_val, cond), F32),
        pltpu.VMEM((1, LANES), F32),
        pltpu.VMEM((2, 2, *block), BF16),
        pltpu.VMEM((2, 2, naux, *block), BF16),
        pltpu.VMEM((2, naux, *block), BF16),
        pltpu.VMEM((2, 2, naux, *block), BF16),
        pltpu.VMEM((2, half, naux_all), BF16),
        pltpu.VMEM((2, peers, half, naux_all), BF16),
        pltpu.VMEM((half, naux_all), F32),
        pltpu.VMEM((half, naux_all), F32),
        pltpu.VMEM((2, ntr, naux, own_val, half * cond), BF16),
        pltpu.VMEM((2, peers, own_val, half * cond), BF16),
        pltpu.VMEM((1, LANES), F32),
        pltpu.VMEM((peers, 1, LANES), F32),
        pltpu.VMEM((2, vectors, LANES), F32),
        pltpu.VMEM((half, own_val, cond), F32),
        pltpu.VMEM((half, own_val, cond), F32),
        dma((7,)),
        dma((2, 2, 2)),
        dma((2, 2)),
        dma((2, 2)),
        dma((2,)),
        dma((8,)),
        dma((8,)),
    ]
    applied, intersection = pl.pallas_call(
        functools.partial(kernel, naux, ntr),
        out_shape=(
            jax.ShapeDtypeStruct((vectors, own_val, cond), F32),
            jax.ShapeDtypeStruct((vectors, vectors), F32),
        ),
        in_specs=[pl.BlockSpec(memory_space=pltpu.SMEM)] + [hbm] * 6,
        out_specs=(vmem, vmem),
        scratch_shapes=scratch,
        compiler_params=pltpu.CompilerParams(
            collective_id=0, has_side_effects=True, vmem_limit_bytes=48 * 1024 * 1024
        ),
    )(
        live_aux, *[pltpu.with_memory_space_constraint(x, pltpu.HBM) for x in (
            trial_vectors, energy_val.reshape(1, -1), energy_cond.reshape(1, -1), coef_occ, coef_virt, pair_coef)]
    )
    return pl.pallas_call(
        finish,
        out_shape=(
            jax.ShapeDtypeStruct(trial_vectors.shape, F32),
            jax.ShapeDtypeStruct((vectors, vectors), F32),
        ),
        in_specs=[vmem, vmem],
        out_specs=(vmem, vmem),
        compiler_params=pltpu.CompilerParams(vmem_limit_bytes=2 * 1024 * 1024),
    )(applied, intersection)


def solution(mesh):
    in_specs = (
        P("aux", None, "tr"),
        P("aux"),
        P("tr"),
        P("aux", None, None),
        P("aux", "tr", None),
        P("aux", "tr", None),
        P("aux"),
    )
    out_specs = (P("aux", None, "tr"), P())
    sizes = (mesh.shape["aux"], mesh.shape["tr"])
    return jax.shard_map(
        functools.partial(body, *sizes), mesh=mesh, in_specs=in_specs, out_specs=out_specs, check_vma=False
    )
```

```python
import contextlib
import functools

import jax
import jax.numpy as jnp
from jax import lax
from jax.experimental import pallas as pl
from jax.experimental.pallas import tpu as pltpu
from jax.sharding import PartitionSpec as P

F32 = jnp.float32
BF16 = jnp.bfloat16
BLEND = 64
LANES = 128
MESH = pl.DeviceIdType.MESH


def scope(name):
    return contextlib.nullcontext()


def kernel(
    naux, ntr,
    live_ref, trial_hbm, val_hbm, cond_hbm, occ_hbm, virt_hbm, pair_hbm,
    out_ref, inter_ref,
    trial_ref, val_ref, cond_ref, occ, virt, pair, blended, acc, mixed, trial_k, own_row,
    block_send, block_recv, cross_recv, mate_recv, proj_send, proj_recv, proj_all, proj_mate,
    sum_send, sum_recv, dots_send, dots_recv, core_recv, final_send, final_recv,
    load_sem, block_sem, proj_sem, sum_sem, dots_sem, extra_ssem, extra_rsem,
):
    g = lax.axis_index("grp")
    a = lax.axis_index("aux")
    t = lax.axis_index("tr")
    own_val, vectors, cond = trial_ref.shape
    half = vectors // 2
    size = half // 2
    slots, val, _ = occ.shape
    here = a * ntr + t

    arrays = ((trial_hbm, trial_ref), (val_hbm, val_ref), (cond_hbm, cond_ref),
              (pair_hbm, pair), (occ_hbm, occ)) + tuple(
        (virt_hbm.at[:, :, pl.ds(pl.multiple_of(lax.rem(t + dt, ntr) * cond, cond), cond)], virt.at[dt])
        for dt in (1, 0))
    loads = [pltpu.make_async_copy(src, dst, load_sem.at[n]) for n, (src, dst) in enumerate(arrays)]
    pair_copy, occ_copy, *virt_copies = loads[3:]
    for copy in loads[:3]:
        copy.start()

    everyone = [(da, dt) for da in reversed(range(naux)) for dt in reversed(range(ntr)) if (da, dt) != (0, 0)]

    assert naux & (naux - 1) == 0
    partners = [a]
    for bit in [1 << i for i in range(naux.bit_length() - 1)]:
        step = bit * (1 - 2 * lax.rem(lax.div(a, bit), 2))
        partners += [p + step for p in partners]
    others = [t] + [lax.rem(t + dt, ntr) for dt in range(1, ntr)]

    def peer(da, dt):
        return {"aux": partners[da], "tr": others[dt]}

    def send(src, dst, ssem, rsem, device):
        return pltpu.make_async_remote_copy(
            src_ref=src, dst_ref=dst, send_sem=ssem, recv_sem=rsem, device_id=device, device_id_type=MESH)

    def drain(refs, sem):
        return pltpu.make_async_copy(refs, refs, sem).wait

    mate = {"grp": 1 - g}
    barrier = pltpu.get_barrier_semaphore()
    with scope("signals"):
        greeted = [peer(da, 0) for da in reversed(range(1, naux))] + [peer(0, dt) for dt in range(1, ntr)] + [mate]
        for device in greeted:
            pl.semaphore_signal(barrier, inc=1, device_id=device, device_id_type=MESH)
    for copy in loads[3:]:
        copy.start()

    with scope("prep"):
        for copy in loads[:3]:
            copy.wait()
        square = (own_val, own_val)
        diagonal = lax.broadcasted_iota(jnp.int32, square, 0) == lax.broadcasted_iota(jnp.int32, square, 1)
        val_column = jnp.sum(jnp.where(diagonal, val_ref[...], 0.0), axis=1, keepdims=True)
        gap = cond_ref[...] - val_column
        for k in range(vectors):
            trial_k[k] = trial_ref[:, k, :]

    pairs = half * vectors
    lane = lax.broadcasted_iota(jnp.int32, (vectors, LANES), 1)
    vector = lax.broadcasted_iota(jnp.int32, (vectors, LANES), 0)

    def fold(x):
        return sum(x[:, n * LANES:(n + 1) * LANES] for n in range(x.shape[1] // LANES))

    def row_of(parts):
        rows = jnp.concatenate([jnp.sum(p, axis=0, keepdims=True) for part in parts for p in part], axis=0)
        n = lax.broadcasted_iota(jnp.int32, (pairs, LANES), 0)
        j = n // vectors
        place = j * vectors + lax.rem(n - j * vectors + g * half, vectors)
        spread = lax.broadcasted_iota(jnp.int32, (pairs, LANES), 1) == place
        return jnp.sum(jnp.where(spread, jnp.sum(rows, axis=1, keepdims=True), 0.0), axis=0, keepdims=True)

    def column(row, j):
        return jnp.sum(jnp.where(lane == j * vectors + vector, row, 0.0), axis=1, keepdims=True)

    def apply(it, vectors_of):
        finals = []

        def go(copy):
            copy.start()
            finals.append(copy.wait_send)
            return copy

        if it == 0:
            with scope("barrier"):
                pl.semaphore_wait(barrier, len(greeted))
        x = []
        with scope("gather_issue"):
            for h in range(2):
                x += vectors_of(h)
                block = jnp.concatenate(x[h * size:], axis=1).astype(BF16)
                block_send[it, h] = block
                block_recv[it, h, a] = block
                for d in reversed(range(1, naux)):
                    send(block_send.at[it, h], block_recv.at[it, h, a],
                         block_sem.at[0, it, h], block_sem.at[1, it, h], peer(d, 0)).start()
                blocks = block_recv.at[it, h, pl.ds(0, naux - 1)]
                finals.append(drain(blocks, block_sem.at[0, it, h]))

        with scope("project"):
            if it == 0:
                pair_copy.wait()
            for k in range(half):
                mixed[:, k, :] = x[k]
            proj = jnp.zeros((half, pair.shape[2]), F32)
            for v in range(own_val):
                proj += jnp.dot(mixed[v].astype(BF16), pair[v], preferred_element_type=F32)
            proj_send[it] = proj.astype(BF16)
            proj_recv[it, here] = proj.astype(BF16)

        if it == 0:
            with scope("mask"):
                occ_copy.wait()
                live = live_ref[0]
                step = min(16, slots)

                @pl.loop(0, slots // step)
                def _(i):
                    for q in range(step):
                        p = i * step + q
                        keep = jnp.full((val, val), jnp.where(p < live, 1.0, 0.0), F32).astype(BF16)
                        occ[p] = occ[p] * keep

                trials = [trial_k[lax.rem(g * half + n, vectors)] for n in range(vectors)]
                own_row[...] = row_of([[fold(gap * trials[j] * trials[n]) for n in range(vectors)] for j in range(half)])

        crosses, mates = [], []
        mate_cross = send(cross_recv, mate_recv.at[1], extra_ssem.at[4], extra_rsem.at[4], mate)
        for h in range(2):
            with scope("gather_wait"):
                drain(block_recv.at[it, h, pl.ds(0, naux - 1)], block_sem.at[1, it, h])()
            if it == 0:
                crosses.append(go(send(
                    block_recv.at[0, h], cross_recv.at[h], extra_ssem.at[h], extra_rsem.at[h], peer(0, 1))))
                mates.append(go(send(
                    block_recv.at[0, h], mate_recv.at[0, h], extra_ssem.at[2 + h], extra_rsem.at[2 + h], mate)))
            if h == 1:
                with scope("proj_issue"):
                    for da, dt in everyone:
                        send(proj_send.at[it], proj_recv.at[it, here], proj_sem.at[0, it], proj_sem.at[1, it],
                             peer(da, dt)).start()
                    projections = proj_recv.at[it, pl.ds(0, len(everyone))]
                    finals.append(drain(projections, proj_sem.at[0, it]))
            with scope("blend"):
                wide = jnp.concatenate([block_recv[it, h, s].astype(F32) for s in range(naux)], axis=0).astype(BF16)
                columns = [wide[:, k * cond:(k + 1) * cond] for k in range(size)]

                @pl.when((t, a)[h] >= 0)
                def _():
                    i = 0
                    rows = occ[pl.ds(i * BLEND, BLEND)].reshape(BLEND * val, val)
                    for k in range(size):
                        b = jnp.dot(rows, columns[k], preferred_element_type=F32).astype(BF16)
                        for q in range(BLEND):
                            blended[i, (h * size + k) * val:(h * size + k + 1) * val,
                                    q * cond:(q + 1) * cond] = b[q * val:(q + 1) * val]

        if it == 0:
            with scope("virt_wait"):
                for copy in virt_copies:
                    copy.wait()

        part = val // 2
        owners = naux // 2

        def contract(rows, dt):
            mixture = jnp.concatenate([
                jnp.concatenate([blended[i, ds, :] for i in range(slots // BLEND)], axis=1) for ds in rows], axis=0)
            acc[:mixture.shape[0]] = jnp.dot(
                mixture, virt[dt].reshape(slots * cond, cond), preferred_element_type=F32)

        def pack(dt, s, rows):
            for k in range(half):
                sum_send[it, dt, s, :, k * cond:(k + 1) * cond] = acc[pl.ds(rows[k], own_val), :].astype(BF16)

        def post(dt, steps):
            for d in reversed(steps):
                send(sum_send.at[it, dt, partners[d]], sum_recv.at[it, dt * naux + d],
                     sum_sem.at[0, it], sum_sem.at[1, it], peer(d, dt)).start()

        with scope("contract_a"):
            @pl.when(g >= 0)
            def _():
                contract([pl.ds(0, half * val)], 1)
                for s in range(naux):
                    pack(1, s, [k * val + s * own_val for k in range(half)])
                post(1, range(naux))
        if it == 0:
            with scope("cross_wait"):
                for copy in crosses:
                    copy.wait_recv()
                mate_cross.start()
            with scope("contract_b"):
                @pl.when(t >= 0)
                def _():
                    contract([pl.ds(0, half * val)], 0)
                    for s in range(naux):
                        pack(0, s, [k * val + s * own_val for k in range(half)])
        else:
            with scope("contract_b"):
                @pl.loop(0, 2)
                def _(h):
                    side = lax.rem(a // owners + 1 + h, 2)
                    contract([
                        pl.ds(pl.multiple_of(k * val + side * part, part), part) for k in range(half)], 0)
                    for s in range(owners):
                        pack(0, side * owners + s, [k * part + s * own_val for k in range(half)])

                    @pl.when(h == 0)
                    def _():
                        post(0, range(owners, naux))

                    @pl.when(h == 1)
                    def _():
                        post(0, range(1, owners))

        with scope("sum_issue"):
            sums = sum_recv.at[it, pl.ds(1, len(everyone))]
            finals.append(drain(sums, sum_sem.at[0, it]))
            if it == 0:
                finals.append(mate_cross.wait_send)

        if it == 0:
            with scope("overlap"):
                for copy in mates:
                    copy.wait_recv()
                mate_cross.wait_recv()
                parts = [[jnp.zeros((own_val, LANES), F32)] * vectors for _ in range(half)]
                for dt in range(2):
                    for s in range(naux):
                        same = block_recv.at[0] if dt == 0 else cross_recv
                        both = [
                            ref[h, s, :, k * cond:(k + 1) * cond].astype(F32)
                            for ref in (same, mate_recv.at[dt]) for h in range(2) for k in range(size)]
                        for j in range(half):
                            mine = sum_send[0, dt, s, :, j * cond:(j + 1) * cond].astype(F32)
                            for n in range(vectors):
                                parts[j][n] = parts[j][n] + fold(mine * both[n])
                row = own_row[...] + row_of(parts)
                dots_send[...] = row
                dots_recv[here] = row
            with scope("dots_issue"):
                for da, dt in everyone:
                    send(dots_send, dots_recv.at[here], dots_sem.at[0], dots_sem.at[1], peer(da, dt)).start()
                post(0, range(1, naux))

        with scope("exchange"):
            drain(projections, proj_sem.at[1, it])()
            proj = proj_recv[it, 0].astype(F32)
            for n in range(1, naux * ntr):
                proj += proj_recv[it, n].astype(F32)
            if it == 0:
                proj_all[...] = proj
                mate_proj = go(send(proj_all, proj_mate, extra_ssem.at[5], extra_rsem.at[5], mate))
            proj_b = proj.astype(BF16)
            for v in range(own_val):
                mixed[v] = lax.dot_general(
                    proj_b, pair[v], (((1,), (1,)), ((), ())), preferred_element_type=F32)
            local = [gap * x[k] + mixed[:, k, :] for k in range(half)]

        exchanged = []
        if it == 0:
            mate_proj.wait_recv()
            both = jnp.concatenate([proj_all[...], proj_mate[...]], axis=0)
            both = jnp.where(g == 0, both, jnp.concatenate([proj_mate[...], proj_all[...]], axis=0))
            exchanged = [
                jnp.sum(fold(both * proj_b[j:j + 1].astype(F32)), axis=1, keepdims=True) for j in range(half)]

        with scope("sum_wait"):
            drain(sums, sum_sem.at[1, it])()
        with scope("combine"):
            total = sum_send[it, 0, a].astype(F32)
            for n in range(1, naux * ntr):
                total += sum_recv[it, n].astype(F32)
            result = [local[k] + total[:, k * cond:(k + 1) * cond] for k in range(half)]
        return result, exchanged, finals

    first, exchanged, finals = apply(0, lambda h: [trial_k[g * half + h * size + k] for k in range(size)])

    with scope("dots_wait"):
        dots = dots_recv.at[pl.ds(0, len(everyone))]
        drain(dots, dots_sem.at[1])()
        finals.append(drain(dots, dots_sem.at[0]))
    with scope("correct"):
        row = dots_recv[0]
        for n in range(1, naux * ntr):
            row += dots_recv[n]
        inter = []
        for j in range(half):
            inter.append((column(row, j) + exchanged[j]) / (naux * own_val * ntr * cond))
    def correction(h):
        corrected = []
        for j in range(h * size, (h + 1) * size):
            fitted = trial_k[0] * inter[j][0:1, :]
            for k in range(1, vectors):
                fitted += trial_k[k] * inter[j][k:k + 1, :]
            corrected.append((first[j] - fitted) / gap)
        return corrected

    second, _, more = apply(1, correction)
    with scope("core_dots"):
        square = jnp.zeros((vectors, LANES), F32)
        for j in range(half):
            square += jnp.where(lane == g * half + j, inter[j], 0.0)
        core_recv[0] = square
        core_dots = send(core_recv.at[0], core_recv.at[1], extra_ssem.at[6], extra_rsem.at[6], mate)
        core_dots.start()
    with scope("final_pack"):
        for k in range(half):
            final_send[k] = second[k]
        final_copy = send(final_send, final_recv, extra_ssem.at[7], extra_rsem.at[7], mate)
        final_copy.start()
        for k in range(half):
            out_ref[g * half + k] = second[k]
    with scope("final_sends"):
        core_dots.wait()
        inter_ref[...] = (core_recv[0] + core_recv[1])[:, :vectors]
        for wait in finals + more:
            wait()
    with scope("final_wait"):
        final_copy.wait()
    with scope("final_store"):
        for k in range(half):
            out_ref[(1 - g) * half + k] = final_recv[k]


def finish(applied_ref, inter_ref, out_ref, inter_out_ref):
    for k in range(applied_ref.shape[0]):
        out_ref[:, k, :] = applied_ref[k]
    inter_out_ref[...] = inter_ref[...]


def body(naux, ntr, trial_vectors, energy_val, energy_cond, coef_occ, coef_virt, pair_coef, live_aux):
    own_val, vectors, cond = trial_vectors.shape
    slots, val, _ = coef_occ.shape
    naux_all = pair_coef.shape[2]
    half = vectors // 2
    peers = naux * ntr
    vmem = pl.BlockSpec(memory_space=pltpu.VMEM)
    hbm = pl.BlockSpec(memory_space=pltpu.HBM)
    dma = pltpu.SemaphoreType.DMA
    block = (own_val, half // 2 * cond)
    scratch = [
        pltpu.VMEM(trial_vectors.shape, F32),
        pltpu.VMEM((1, own_val), F32),
        pltpu.VMEM((1, cond), F32),
        pltpu.VMEM(coef_occ.shape, BF16),
        pltpu.VMEM((ntr, slots, cond, cond), BF16),
        pltpu.VMEM(pair_coef.shape, BF16),
        pltpu.VMEM((slots // BLEND, half * val, BLEND * cond), BF16),
        pltpu.VMEM((half * val, cond), F32),
        pltpu.VMEM((own_val, half, cond), F32),
        pltpu.VMEM((vectors, own_val, cond), F32),
        pltpu.VMEM((1, LANES), F32),
        pltpu.VMEM((2, 2, *block), BF16),
        pltpu.VMEM((2, 2, naux, *block), BF16),
        pltpu.VMEM((2, naux, *block), BF16),
        pltpu.VMEM((2, 2, naux, *block), BF16),
        pltpu.VMEM((2, half, naux_all), BF16),
        pltpu.VMEM((2, peers, half, naux_all), BF16),
        pltpu.VMEM((half, naux_all), F32),
        pltpu.VMEM((half, naux_all), F32),
        pltpu.VMEM((2, ntr, naux, own_val, half * cond), BF16),
        pltpu.VMEM((2, peers, own_val, half * cond), BF16),
        pltpu.VMEM((1, LANES), F32),
        pltpu.VMEM((peers, 1, LANES), F32),
        pltpu.VMEM((2, vectors, LANES), F32),
        pltpu.VMEM((half, own_val, cond), F32),
        pltpu.VMEM((half, own_val, cond), F32),
        dma((7,)),
        dma((2, 2, 2)),
        dma((2, 2)),
        dma((2, 2)),
        dma((2,)),
        dma((8,)),
        dma((8,)),
    ]
    applied, intersection = pl.pallas_call(
        functools.partial(kernel, naux, ntr),
        out_shape=(
            jax.ShapeDtypeStruct((vectors, own_val, cond), F32),
            jax.ShapeDtypeStruct((vectors, vectors), F32),
        ),
        in_specs=[pl.BlockSpec(memory_space=pltpu.SMEM)] + [hbm] * 6,
        out_specs=(vmem, vmem),
        scratch_shapes=scratch,
        compiler_params=pltpu.CompilerParams(
            collective_id=0, has_side_effects=True, vmem_limit_bytes=48 * 1024 * 1024
        ),
    )(
        live_aux, *[pltpu.with_memory_space_constraint(x, pltpu.HBM) for x in (
            trial_vectors, energy_val.reshape(1, -1), energy_cond.reshape(1, -1), coef_occ, coef_virt, pair_coef)]
    )
    return pl.pallas_call(
        finish,
        out_shape=(
            jax.ShapeDtypeStruct(trial_vectors.shape, F32),
            jax.ShapeDtypeStruct((vectors, vectors), F32),
        ),
        in_specs=[vmem, vmem],
        out_specs=(vmem, vmem),
        compiler_params=pltpu.CompilerParams(vmem_limit_bytes=2 * 1024 * 1024),
    )(applied, intersection)


def solution(mesh):
    in_specs = (
        P("aux", None, "tr"),
        P("aux"),
        P("tr"),
        P("aux", None, None),
        P("aux", "tr", None),
        P("aux", "tr", None),
        P("aux"),
    )
    out_specs = (P("aux", None, "tr"), P())
    sizes = (mesh.shape["aux"], mesh.shape["tr"])
    return jax.shard_map(
        functools.partial(body, *sizes), mesh=mesh, in_specs=in_specs, out_specs=out_specs, check_vma=False
    )
```

```python
import contextlib
import functools

import jax
import jax.numpy as jnp
from jax import lax
from jax.experimental import pallas as pl
from jax.experimental.pallas import tpu as pltpu
from jax.sharding import PartitionSpec as P

F32 = jnp.float32
BF16 = jnp.bfloat16
BLEND = 64
LANES = 128
MESH = pl.DeviceIdType.MESH


def scope(name):
    return contextlib.nullcontext()


def kernel(
    naux, ntr,
    live_ref, trial_hbm, val_hbm, cond_hbm, occ_hbm, virt_hbm, pair_hbm,
    out_ref, inter_ref,
    trial_ref, val_ref, cond_ref, occ, virt, pair, blended, acc, mixed, trial_k, own_row,
    block_send, block_recv, cross_recv, mate_recv, proj_send, proj_recv, proj_all, proj_mate,
    sum_send, sum_recv, dots_send, dots_recv, core_recv, final_send, final_recv,
    load_sem, block_sem, proj_sem, sum_sem, dots_sem, extra_ssem, extra_rsem,
):
    g = lax.axis_index("grp")
    a = lax.axis_index("aux")
    t = lax.axis_index("tr")
    own_val, vectors, cond = trial_ref.shape
    half = vectors // 2
    size = half // 2
    slots, val, _ = occ.shape
    here = a * ntr + t

    arrays = ((trial_hbm, trial_ref), (val_hbm, val_ref), (cond_hbm, cond_ref),
              (pair_hbm, pair), (occ_hbm, occ)) + tuple(
        (virt_hbm.at[:, :, pl.ds(pl.multiple_of(lax.rem(t + dt, ntr) * cond, cond), cond)], virt.at[dt])
        for dt in (1, 0))
    loads = [pltpu.make_async_copy(src, dst, load_sem.at[n]) for n, (src, dst) in enumerate(arrays)]
    pair_copy, occ_copy, *virt_copies = loads[3:]
    for copy in loads[:3]:
        copy.start()

    everyone = [(da, dt) for da in reversed(range(naux)) for dt in reversed(range(ntr)) if (da, dt) != (0, 0)]

    assert naux & (naux - 1) == 0
    partners = [a]
    for bit in [1 << i for i in range(naux.bit_length() - 1)]:
        step = bit * (1 - 2 * lax.rem(lax.div(a, bit), 2))
        partners += [p + step for p in partners]
    others = [t] + [lax.rem(t + dt, ntr) for dt in range(1, ntr)]

    def peer(da, dt):
        return {"aux": partners[da], "tr": others[dt]}

    def send(src, dst, ssem, rsem, device):
        return pltpu.make_async_remote_copy(
            src_ref=src, dst_ref=dst, send_sem=ssem, recv_sem=rsem, device_id=device, device_id_type=MESH)

    def drain(refs, sem):
        return pltpu.make_async_copy(refs, refs, sem).wait

    mate = {"grp": 1 - g}
    barrier = pltpu.get_barrier_semaphore()
    with scope("signals"):
        greeted = [peer(da, 0) for da in reversed(range(1, naux))] + [peer(0, dt) for dt in range(1, ntr)] + [mate]
        for device in greeted:
            pl.semaphore_signal(barrier, inc=1, device_id=device, device_id_type=MESH)
    for copy in loads[3:]:
        copy.start()

    with scope("prep"):
        for copy in loads[:3]:
            copy.wait()
        square = (own_val, own_val)
        diagonal = lax.broadcasted_iota(jnp.int32, square, 0) == lax.broadcasted_iota(jnp.int32, square, 1)
        val_column = jnp.sum(jnp.where(diagonal, val_ref[...], 0.0), axis=1, keepdims=True)
        gap = cond_ref[...] - val_column
        for k in range(vectors):
            trial_k[k] = trial_ref[:, k, :]

    pairs = half * vectors
    lane = lax.broadcasted_iota(jnp.int32, (vectors, LANES), 1)
    vector = lax.broadcasted_iota(jnp.int32, (vectors, LANES), 0)

    def fold(x):
        return sum(x[:, n * LANES:(n + 1) * LANES] for n in range(x.shape[1] // LANES))

    def row_of(parts):
        rows = jnp.concatenate([jnp.sum(p, axis=0, keepdims=True) for part in parts for p in part], axis=0)
        n = lax.broadcasted_iota(jnp.int32, (pairs, LANES), 0)
        j = n // vectors
        place = j * vectors + lax.rem(n - j * vectors + g * half, vectors)
        spread = lax.broadcasted_iota(jnp.int32, (pairs, LANES), 1) == place
        return jnp.sum(jnp.where(spread, jnp.sum(rows, axis=1, keepdims=True), 0.0), axis=0, keepdims=True)

    def column(row, j):
        return jnp.sum(jnp.where(lane == j * vectors + vector, row, 0.0), axis=1, keepdims=True)

    def apply(it, vectors_of):
        finals = []

        def go(copy):
            copy.start()
            finals.append(copy.wait_send)
            return copy

        if it == 0:
            with scope("barrier"):
                pl.semaphore_wait(barrier, len(greeted))
        x = []
        with scope("gather_issue"):
            for h in range(2):
                x += vectors_of(h)
                block = jnp.concatenate(x[h * size:], axis=1).astype(BF16)
                block_send[it, h] = block
                block_recv[it, h, a] = block
                for d in reversed(range(1, naux)):
                    send(block_send.at[it, h], block_recv.at[it, h, a],
                         block_sem.at[0, it, h], block_sem.at[1, it, h], peer(d, 0)).start()
                blocks = block_recv.at[it, h, pl.ds(0, naux - 1)]
                finals.append(drain(blocks, block_sem.at[0, it, h]))

        with scope("project"):
            if it == 0:
                pair_copy.wait()
            for k in range(half):
                mixed[:, k, :] = x[k]
            proj = jnp.zeros((half, pair.shape[2]), F32)
            for v in range(own_val):
                proj += jnp.dot(mixed[v].astype(BF16), pair[v], preferred_element_type=F32)
            proj_send[it] = proj.astype(BF16)
            proj_recv[it, here] = proj.astype(BF16)

        if it == 0:
            with scope("mask"):
                occ_copy.wait()
                live = live_ref[0]
                step = min(16, slots)

                @pl.loop(0, slots // step)
                def _(i):
                    for q in range(step):
                        p = i * step + q
                        keep = jnp.full((val, val), jnp.where(p < live, 1.0, 0.0), F32).astype(BF16)
                        occ[p] = occ[p] * keep

                trials = [trial_k[lax.rem(g * half + n, vectors)] for n in range(vectors)]
                own_row[...] = row_of([[fold(gap * trials[j] * trials[n]) for n in range(vectors)] for j in range(half)])

        mate_cross = send(cross_recv, mate_recv.at[1], extra_ssem.at[2], extra_rsem.at[2], mate)
        for h in range(2):
            with scope("gather_wait"):
                drain(block_recv.at[it, h, pl.ds(0, naux - 1)], block_sem.at[1, it, h])()
            if it == 0:
                send(block_recv.at[0, h], cross_recv.at[h], extra_ssem.at[0], extra_rsem.at[0], peer(0, 1)).start()
                send(block_recv.at[0, h], mate_recv.at[0, h], extra_ssem.at[1], extra_rsem.at[1], mate).start()
            if h == 1:
                with scope("proj_issue"):
                    for da, dt in everyone:
                        send(proj_send.at[it], proj_recv.at[it, here], proj_sem.at[0, it], proj_sem.at[1, it],
                             peer(da, dt)).start()
                    projections = proj_recv.at[it, pl.ds(0, len(everyone))]
                    finals.append(drain(projections, proj_sem.at[0, it]))
            with scope("blend"):
                wide = jnp.concatenate([block_recv[it, h, s].astype(F32) for s in range(naux)], axis=0).astype(BF16)
                columns = [wide[:, k * cond:(k + 1) * cond] for k in range(size)]

                @pl.when((t, a)[h] >= 0)
                def _():
                    i = 0
                    rows = occ[pl.ds(i * BLEND, BLEND)].reshape(BLEND * val, val)
                    for k in range(size):
                        b = jnp.dot(rows, columns[k], preferred_element_type=F32).astype(BF16)
                        for q in range(BLEND):
                            blended[i, (h * size + k) * val:(h * size + k + 1) * val,
                                    q * cond:(q + 1) * cond] = b[q * val:(q + 1) * val]

        if it == 0:
            with scope("virt_wait"):
                for copy in virt_copies:
                    copy.wait()

        part = val // 2
        owners = naux // 2

        def contract(rows, dt):
            mixture = jnp.concatenate([
                jnp.concatenate([blended[i, ds, :] for i in range(slots // BLEND)], axis=1) for ds in rows], axis=0)
            acc[:mixture.shape[0]] = jnp.dot(
                mixture, virt[dt].reshape(slots * cond, cond), preferred_element_type=F32)

        def pack(dt, s, rows):
            for k in range(half):
                sum_send[it, dt, s, :, k * cond:(k + 1) * cond] = acc[pl.ds(rows[k], own_val), :].astype(BF16)

        def post(dt, steps):
            for d in reversed(steps):
                send(sum_send.at[it, dt, partners[d]], sum_recv.at[it, dt * naux + d],
                     sum_sem.at[0, it], sum_sem.at[1, it], peer(d, dt)).start()

        with scope("contract_a"):
            @pl.when(g >= 0)
            def _():
                contract([pl.ds(0, half * val)], 1)
                for s in range(naux):
                    pack(1, s, [k * val + s * own_val for k in range(half)])
                post(1, range(naux))
        if it == 0:
            with scope("cross_wait"):
                drain(cross_recv, extra_rsem.at[0])()
                finals.append(drain(cross_recv, extra_ssem.at[0]))
                mate_cross.start()
            with scope("contract_b"):
                @pl.when(t >= 0)
                def _():
                    contract([pl.ds(0, half * val)], 0)
                    for s in range(naux):
                        pack(0, s, [k * val + s * own_val for k in range(half)])
        else:
            with scope("contract_b"):
                @pl.loop(0, 2)
                def _(h):
                    side = lax.rem(a // owners + 1 + h, 2)
                    contract([
                        pl.ds(pl.multiple_of(k * val + side * part, part), part) for k in range(half)], 0)
                    for s in range(owners):
                        pack(0, side * owners + s, [k * part + s * own_val for k in range(half)])

                    @pl.when(h == 0)
                    def _():
                        post(0, range(owners, naux))

                    @pl.when(h == 1)
                    def _():
                        post(0, range(1, owners))

        with scope("sum_issue"):
            sums = sum_recv.at[it, pl.ds(1, len(everyone))]
            finals.append(drain(sums, sum_sem.at[0, it]))
            if it == 0:
                finals.append(mate_cross.wait_send)

        if it == 0:
            with scope("overlap"):
                drain(mate_recv.at[0], extra_rsem.at[1])()
                finals.append(drain(mate_recv.at[0], extra_ssem.at[1]))
                mate_cross.wait_recv()
                parts = [[jnp.zeros((own_val, LANES), F32)] * vectors for _ in range(half)]
                for dt in range(2):
                    for s in range(naux):
                        same = block_recv.at[0] if dt == 0 else cross_recv
                        both = [
                            ref[h, s, :, k * cond:(k + 1) * cond].astype(F32)
                            for ref in (same, mate_recv.at[dt]) for h in range(2) for k in range(size)]
                        for j in range(half):
                            mine = sum_send[0, dt, s, :, j * cond:(j + 1) * cond].astype(F32)
                            for n in range(vectors):
                                parts[j][n] = parts[j][n] + fold(mine * both[n])
                row = own_row[...] + row_of(parts)
                dots_send[...] = row
                dots_recv[here] = row
            with scope("dots_issue"):
                for da, dt in everyone:
                    send(dots_send, dots_recv.at[here], dots_sem.at[0], dots_sem.at[1], peer(da, dt)).start()
                post(0, range(1, naux))

        with scope("exchange"):
            drain(projections, proj_sem.at[1, it])()
            proj = proj_recv[it, 0].astype(F32)
            for n in range(1, naux * ntr):
                proj += proj_recv[it, n].astype(F32)
            if it == 0:
                proj_all[...] = proj
                mate_proj = go(send(proj_all, proj_mate, extra_ssem.at[3], extra_rsem.at[3], mate))
            proj_b = proj.astype(BF16)
            for v in range(own_val):
                mixed[v] = lax.dot_general(
                    proj_b, pair[v], (((1,), (1,)), ((), ())), preferred_element_type=F32)
            local = [gap * x[k] + mixed[:, k, :] for k in range(half)]

        exchanged = []
        if it == 0:
            mate_proj.wait_recv()
            both = jnp.concatenate([proj_all[...], proj_mate[...]], axis=0)
            both = jnp.where(g == 0, both, jnp.concatenate([proj_mate[...], proj_all[...]], axis=0))
            exchanged = [
                jnp.sum(fold(both * proj_b[j:j + 1].astype(F32)), axis=1, keepdims=True) for j in range(half)]

        with scope("sum_wait"):
            drain(sums, sum_sem.at[1, it])()
        with scope("combine"):
            total = sum_send[it, 0, a].astype(F32)
            for n in range(1, naux * ntr):
                total += sum_recv[it, n].astype(F32)
            result = [local[k] + total[:, k * cond:(k + 1) * cond] for k in range(half)]
        return result, exchanged, finals

    first, exchanged, finals = apply(0, lambda h: [trial_k[g * half + h * size + k] for k in range(size)])

    with scope("dots_wait"):
        dots = dots_recv.at[pl.ds(0, len(everyone))]
        drain(dots, dots_sem.at[1])()
        finals.append(drain(dots, dots_sem.at[0]))
    with scope("correct"):
        row = dots_recv[0]
        for n in range(1, naux * ntr):
            row += dots_recv[n]
        inter = []
        for j in range(half):
            inter.append((column(row, j) + exchanged[j]) / (naux * own_val * ntr * cond))
    def correction(h):
        corrected = []
        for j in range(h * size, (h + 1) * size):
            fitted = trial_k[0] * inter[j][0:1, :]
            for k in range(1, vectors):
                fitted += trial_k[k] * inter[j][k:k + 1, :]
            corrected.append((first[j] - fitted) / gap)
        return corrected

    second, _, more = apply(1, correction)
    with scope("core_dots"):
        square = jnp.zeros((vectors, LANES), F32)
        for j in range(half):
            square += jnp.where(lane == g * half + j, inter[j], 0.0)
        core_recv[0] = square
        core_dots = send(core_recv.at[0], core_recv.at[1], extra_ssem.at[4], extra_rsem.at[4], mate)
        core_dots.start()
    with scope("final_pack"):
        for k in range(half):
            final_send[k] = second[k]
        final_copy = send(final_send, final_recv, extra_ssem.at[5], extra_rsem.at[5], mate)
        final_copy.start()
        for k in range(half):
            out_ref[g * half + k] = second[k]
    with scope("final_sends"):
        core_dots.wait()
        inter_ref[...] = (core_recv[0] + core_recv[1])[:, :vectors]
        for wait in finals + more:
            wait()
    with scope("final_wait"):
        final_copy.wait()
    with scope("final_store"):
        for k in range(half):
            out_ref[(1 - g) * half + k] = final_recv[k]


def finish(applied_ref, inter_ref, out_ref, inter_out_ref):
    for k in range(applied_ref.shape[0]):
        out_ref[:, k, :] = applied_ref[k]
    inter_out_ref[...] = inter_ref[...]


def body(naux, ntr, trial_vectors, energy_val, energy_cond, coef_occ, coef_virt, pair_coef, live_aux):
    own_val, vectors, cond = trial_vectors.shape
    slots, val, _ = coef_occ.shape
    naux_all = pair_coef.shape[2]
    half = vectors // 2
    peers = naux * ntr
    vmem = pl.BlockSpec(memory_space=pltpu.VMEM)
    hbm = pl.BlockSpec(memory_space=pltpu.HBM)
    dma = pltpu.SemaphoreType.DMA
    block = (own_val, half // 2 * cond)
    scratch = [
        pltpu.VMEM(trial_vectors.shape, F32),
        pltpu.VMEM((1, own_val), F32),
        pltpu.VMEM((1, cond), F32),
        pltpu.VMEM(coef_occ.shape, BF16),
        pltpu.VMEM((ntr, slots, cond, cond), BF16),
        pltpu.VMEM(pair_coef.shape, BF16),
        pltpu.VMEM((slots // BLEND, half * val, BLEND * cond), BF16),
        pltpu.VMEM((half * val, cond), F32),
        pltpu.VMEM((own_val, half, cond), F32),
        pltpu.VMEM((vectors, own_val, cond), F32),
        pltpu.VMEM((1, LANES), F32),
        pltpu.VMEM((2, 2, *block), BF16),
        pltpu.VMEM((2, 2, naux, *block), BF16),
        pltpu.VMEM((2, naux, *block), BF16),
        pltpu.VMEM((2, 2, naux, *block), BF16),
        pltpu.VMEM((2, half, naux_all), BF16),
        pltpu.VMEM((2, peers, half, naux_all), BF16),
        pltpu.VMEM((half, naux_all), F32),
        pltpu.VMEM((half, naux_all), F32),
        pltpu.VMEM((2, ntr, naux, own_val, half * cond), BF16),
        pltpu.VMEM((2, peers, own_val, half * cond), BF16),
        pltpu.VMEM((1, LANES), F32),
        pltpu.VMEM((peers, 1, LANES), F32),
        pltpu.VMEM((2, vectors, LANES), F32),
        pltpu.VMEM((half, own_val, cond), F32),
        pltpu.VMEM((half, own_val, cond), F32),
        dma((7,)),
        dma((2, 2, 2)),
        dma((2, 2)),
        dma((2, 2)),
        dma((2,)),
        dma((6,)),
        dma((6,)),
    ]
    applied, intersection = pl.pallas_call(
        functools.partial(kernel, naux, ntr),
        out_shape=(
            jax.ShapeDtypeStruct((vectors, own_val, cond), F32),
            jax.ShapeDtypeStruct((vectors, vectors), F32),
        ),
        in_specs=[pl.BlockSpec(memory_space=pltpu.SMEM)] + [hbm] * 6,
        out_specs=(vmem, vmem),
        scratch_shapes=scratch,
        compiler_params=pltpu.CompilerParams(
            collective_id=0, has_side_effects=True, vmem_limit_bytes=48 * 1024 * 1024
        ),
    )(
        live_aux, *[pltpu.with_memory_space_constraint(x, pltpu.HBM) for x in (
            trial_vectors, energy_val.reshape(1, -1), energy_cond.reshape(1, -1), coef_occ, coef_virt, pair_coef)]
    )
    return pl.pallas_call(
        finish,
        out_shape=(
            jax.ShapeDtypeStruct(trial_vectors.shape, F32),
            jax.ShapeDtypeStruct((vectors, vectors), F32),
        ),
        in_specs=[vmem, vmem],
        out_specs=(vmem, vmem),
        compiler_params=pltpu.CompilerParams(vmem_limit_bytes=2 * 1024 * 1024),
    )(applied, intersection)


def solution(mesh):
    in_specs = (
        P("aux", None, "tr"),
        P("aux"),
        P("tr"),
        P("aux", None, None),
        P("aux", "tr", None),
        P("aux", "tr", None),
        P("aux"),
    )
    out_specs = (P("aux", None, "tr"), P())
    sizes = (mesh.shape["aux"], mesh.shape["tr"])
    return jax.shard_map(
        functools.partial(body, *sizes), mesh=mesh, in_specs=in_specs, out_specs=out_specs, check_vma=False
    )
```
